128 devices in a mesh: cuts: 8 (over y, core), fsdp: 16 (over z, x).
Axes of the slice: x: 4, y: 4, z: 4, core: 2. Of those that a mesh axis runs over, the one named last changes fastest.
Arguments:
- hidden_states: bfloat16 [65536, 8192], P(('cuts', 'fsdp')), may hold values from -1200 to 1200
- key_cotangent: bfloat16 [65536, 512], P(('cuts', 'fsdp')), may hold values from -60 to 60
- old_weight: bfloat16 [16384, 256], P(('cuts', 'fsdp')), may hold values from -0.0625 to 0.0625
- old_first: bfloat16 [16384, 256], P(('cuts', 'fsdp')), may hold values from -1 to 1
- old_first_scale: float32 [16384], P(('cuts', 'fsdp')), may hold values from 3e-05 to 0.0003
- old_second: bfloat16 [16384, 256], P(('cuts', 'fsdp')), may hold values from 0 to 1
- old_second_scale: float32 [16384], P(('cuts', 'fsdp')), may hold values from 1e-08 to 1e-07
- send_counts: int32 [128, 128], P(('cuts', 'fsdp')), may hold values from 0 to 2, as said below
Outputs:
- input_grad: bfloat16 [65536, 8192], P(('cuts', 'fsdp'))
- new_weight: bfloat16 [8192, 512], P(('cuts', 'fsdp'))
- first_code: bfloat16 [8192, 512], P(('cuts', 'fsdp'))
- first_scale: float32 [8192, 2], P(('cuts', 'fsdp'))
- second_code: bfloat16 [8192, 512], P(('cuts', 'fsdp'))
- second_scale: float32 [8192, 2], P(('cuts', 'fsdp'))
The draws below stay inside these ranges and needn't reach their ends.
Inputs may be any that keep to these rules, and one draw needn't show every extreme that they name: Every row and every column of send_counts sums to 128; each entry is 0, 1 or 2, and every row and every column holds 2 exactly once.
All inputs are finite; a program needn't handle non-finite values.
Results may differ from the reference program's by a relative error of at most 0.00075.
Values may be sent and summed in bfloat16 or wider, within the bound.
A program may use at most 128 MiB of HBM per device.

```python
import math
import jax
import jax.numpy as jnp
from jax import lax

D = 8192
QB = 256
TOK_DEV = 512
STEP = 2000
PEERS = 128
KW = 512
TOKENS = 65536
NB = 16384
NBD = 128
RC = 64
BPR = 2


def draw_hidden_states(key, part):
    key_base, key_rough, key_pair = jax.random.split(jax.random.fold_in(key, 11), 3)
    feature = jnp.arange(D, dtype=jnp.float32) / D
    rough = jnp.exp(jax.random.uniform(key_rough, (D,), jnp.float32, 0.0, math.log(3.3)))
    values = jnp.clip(jax.random.normal(key_base, (TOKENS, D), jnp.float32), -6.0, 6.0)
    rising = jnp.exp(math.log(3.0) * feature)
    pairing = jax.random.permutation(key_pair, PEERS)
    holder = jnp.arange(TOKENS, dtype=jnp.int32) // TOK_DEV
    feature_owner = jnp.arange(D, dtype=jnp.int32) // RC
    paired = pairing[holder][:, None] == feature_owner[None, :]
    spike = jnp.where(paired, 8.0, 1.0)
    return (values * rising[None, :] * rough[None, :] * spike).astype(jnp.bfloat16)


def draw_key_cotangent(key, part):
    key_base, key_scale = jax.random.split(jax.random.fold_in(key, 23), 2)
    values = jnp.clip(jax.random.normal(key_base, (TOKENS, KW), jnp.float32), -6.0, 6.0)
    column_scale = jnp.exp(jax.random.uniform(key_scale, (KW,), jnp.float32, 0.0, math.log(10.0)))
    return (values * column_scale[None, :]).astype(jnp.bfloat16)


def draw_send_counts(key, part):
    key_perm, key_shift = jax.random.split(jax.random.fold_in(key, 37), 2)
    base_count = NBD // PEERS
    ordering = jax.random.permutation(key_perm, PEERS)
    shift_by = jax.random.randint(key_shift, (), 1, PEERS)
    index = jnp.arange(PEERS, dtype=jnp.int32)
    second_order = ordering[(index + shift_by) % PEERS]
    columns = jnp.arange(PEERS, dtype=jnp.int32)[None, :]
    raised = (ordering[:, None] == columns).astype(jnp.int32)
    lowered = (second_order[:, None] == columns).astype(jnp.int32)
    return (base_count + base_count * raised - base_count * lowered).astype(jnp.int32)


def shard_levels(rng, shape, cuts, least, largest):
    loudness, own = 1.0, jax.random.fold_in(rng, 6)
    for dim, parts in cuts:
        draws = jnp.exp(jax.random.uniform(jax.random.fold_in(own, dim), (parts,), jnp.float32, least / len(cuts), largest / len(cuts)))
        loudness = loudness * jnp.repeat(draws, shape[dim] // parts).reshape([-1 if axis == dim else 1 for axis in range(len(shape))])
    return loudness


def normal_values(rng, shape, deviation, most, cuts=(), kind=jnp.bfloat16):
    drawn = deviation * jax.random.normal(rng, shape, jnp.float32)
    if cuts:
        drawn = drawn * shard_levels(rng, shape, cuts, -0.22, 0.18)
    return jnp.clip(drawn, -most, most).astype(kind)


def setup_inputs(seed: int = 0) -> dict:
    seeds = jax.random.split(jax.random.key(seed), 9)
    return {
        "hidden_states": draw_hidden_states(jax.random.fold_in(seeds[8], 71), 0),
        "key_cotangent": draw_key_cotangent(jax.random.fold_in(seeds[8], 71), 0),
        "old_weight": normal_values(seeds[2], (PEERS * NBD, QB), D ** -0.5, 0.0625, ((0, 128),)),
        "old_first": jnp.clip(jax.random.uniform(seeds[3], (PEERS * NBD, QB), jnp.float32, -1.0, 1.0) * shard_levels(seeds[3], (PEERS * NBD, QB), ((0, 128),), -0.4, 0.0), -1.0, 1.0).astype(jnp.bfloat16),
        "old_first_scale": jnp.clip(jnp.exp(math.log(0.0003) - 2.3025852 * jax.random.uniform(seeds[4], (PEERS * NBD,), jnp.float32) ** shard_levels(seeds[4], (PEERS * NBD,), ((0, 128),), -0.2, 0.2)), 2.9999999242136255e-05, 0.0003),
        "old_second": jnp.clip(1.0 * jax.random.uniform(seeds[5], (PEERS * NBD, QB), jnp.float32) ** shard_levels(seeds[5], (PEERS * NBD, QB), ((0, 128),), -0.2, 0.2), 0.0, 1.0).astype(jnp.bfloat16),
        "old_second_scale": jnp.clip(jnp.exp(math.log(1.0000000116860974e-07) - 2.3025851 * jax.random.uniform(seeds[6], (PEERS * NBD,), jnp.float32) ** shard_levels(seeds[6], (PEERS * NBD,), ((0, 128),), -0.2, 0.2)), 9.99999993922529e-09, 1.0000000116860974e-07),
        "send_counts": draw_send_counts(jax.random.fold_in(seeds[8], 71), 0),
    }


beta_first = 0.9
beta_second = 0.95
adam_epsilon = 1e-05
learn_rate = 0.001
weight_decay = 0.1
clip_norm = 1.0
tiny_scale = 1e-30

def reshard(counts, blocks):
    peer_count = counts.shape[0]
    slot_count = blocks.shape[0] // peer_count
    slot_ends = jnp.cumsum(counts, axis=1).astype(jnp.int32)
    starts = slot_ends - counts
    offsets = jnp.cumsum(counts, axis=0).astype(jnp.int32) - counts
    slot_index = jnp.arange(slot_count, dtype=jnp.int32)
    owner = lax.optimization_barrier(jnp.sum((slot_ends[:, None, :] <= slot_index[None, :, None]).astype(jnp.int32), axis=2)).astype(jnp.int32)
    first_slot = jnp.take_along_axis(starts, owner, axis=1)
    base_slot = jnp.take_along_axis(offsets, owner, axis=1)
    target = (owner * slot_count + base_slot + slot_index[None, :] - first_slot).astype(jnp.int32)
    return jnp.zeros_like(blocks).at[target.reshape(-1)].set(blocks)

def adam_blocks(clipped, weight, first, first_scale, second, second_scale):
    m_old = first.astype(jnp.float32) * first_scale[:, None]
    v_old = second.astype(jnp.float32) * second_scale[:, None]
    m_new = beta_first * m_old + (1.0 - beta_first) * clipped
    v_new = beta_second * v_old + (1.0 - beta_second) * clipped * clipped
    m_hat = m_new / (1.0 - beta_first ** STEP)
    v_hat = v_new / (1.0 - beta_second ** STEP)
    w_old = weight.astype(jnp.float32)
    w_new = (w_old - learn_rate * (m_hat / (jnp.sqrt(v_hat) + adam_epsilon) + weight_decay * w_old)).astype(jnp.bfloat16)
    m_scale = lax.optimization_barrier(jnp.max(jnp.abs(m_new), axis=1)) + tiny_scale
    v_scale = lax.optimization_barrier(jnp.max(v_new, axis=1)) + tiny_scale
    m_code = (m_new / m_scale[:, None]).astype(jnp.bfloat16)
    v_code = (v_new / v_scale[:, None]).astype(jnp.bfloat16)
    return (w_new, m_code, m_scale, v_code, v_scale)

def reference(hidden_states, key_cotangent, old_weight, old_first, old_first_scale, old_second, old_second_scale, send_counts):
    weight_blocks = reshard(send_counts, old_weight)
    first_blocks = reshard(send_counts, old_first)
    second_blocks = reshard(send_counts, old_second)
    first_scales = reshard(send_counts, old_first_scale)
    second_scales = reshard(send_counts, old_second_scale)
    full_weight = weight_blocks.reshape(D, KW)
    input_grad = lax.dot_general(key_cotangent, full_weight, (((1,), (1,)), ((), ())), preferred_element_type=jnp.float32).astype(jnp.bfloat16)
    gradient = lax.dot_general(hidden_states, key_cotangent, (((0,), (0,)), ((), ())), preferred_element_type=jnp.float32) / TOKENS
    norm_value = jnp.sqrt(jnp.sum(gradient * gradient))
    factor = jnp.minimum(1.0, clip_norm / (norm_value + 1e-06))
    clipped = (gradient * factor).reshape(NB, QB)
    w_new, m_code, m_scale, v_code, v_scale = adam_blocks(clipped, weight_blocks, first_blocks, first_scales, second_blocks, second_scales)
    return (input_grad, w_new.reshape(D, KW), m_code.reshape(D, KW), m_scale.reshape(D, BPR), v_code.reshape(D, KW), v_scale.reshape(D, BPR))
```

```python
import jax
import jax.numpy as jnp
from jax import lax
from jax.experimental import pallas as pl
from jax.experimental.pallas import tpu as pltpu
from jax.sharding import PartitionSpec as P

STEP = 2000

beta_first = 0.9
beta_second = 0.95
adam_epsilon = 1e-05
learn_rate = 0.001
weight_decay = 0.1
clip_norm = 1.0
tiny_scale = 1e-30

AXES = ("cuts", "fsdp")
MESH = pl.DeviceIdType.MESH
ROWS = (88, 88, 80)
FIRST = (0, 88, 176)
ORDER = ((0, 1, 2), (1, 2, 0), (2, 0, 1))
SPLIT = (48, 48, 40)


def add_into(target, parts):
    outer, inner = target.shape[:2]

    def body(i, carry):
        a, b = i // inner, i % inner
        total = target[a, b]
        for part in parts:
            total = total + part[a, b]
        target[a, b] = total
        return carry

    lax.fori_loop(0, outer * inner, body, 0)


def main_kernel(
    hidden,
    cotangent,
    weight,
    first,
    second,
    scales,
    w_out,
    m_out,
    ms_out,
    v_out,
    vs_out,
    h_own,
    h_pair,
    c_own,
    c_pair,
    b0,
    b1,
    b2,
    f0,
    f1,
    f2,
    n0,
    n1,
    n2,
    grad,
    plane,
    line,
    load_sem,
    pair_send,
    pair_recv,
    ring_send,
    ring_recv,
    sum_send,
    sum_recv,
):
    cut = lax.axis_index("cuts")
    fs = lax.axis_index("fsdp")
    y, core = cut // 2, cut % 2
    z, x = fs // 4, fs % 4
    here = (y, z, x)

    def at(y, z, x, core):
        return (y * 2 + core, z * 4 + x)

    def neighbour(axis, step):
        place = list(here)
        place[axis] = (place[axis] + step) % 4
        return at(*place, core)

    partner = at(y, z, x, 1 - core)

    order = [(y + s) % 4 for s in (2, 1, 3, 0)]
    loads = [pltpu.make_async_copy(cotangent, c_own, load_sem.at[4])]
    loads[0].start()
    for i, yy in enumerate(order):
        cols = pl.multiple_of(yy * 2048 + core * 1024, 1024)
        copy = pltpu.make_async_copy(hidden.at[:, pl.ds(cols, 1024)], h_own.at[i], load_sem.at[i])
        copy.start()
        loads.append(copy)

    barrier = pltpu.get_barrier_semaphore()
    for s in range(1, 16):
        pl.semaphore_signal(barrier, inc=1, device_id=(cut, (fs + s) % 16), device_id_type=MESH)
    for s in range(1, 8):
        pl.semaphore_signal(barrier, inc=1, device_id=((cut + s) % 8, fs), device_id_type=MESH)
    pl.semaphore_wait(barrier, 22)

    def remote(src, dst, send, recv, device):
        return pltpu.make_async_remote_copy(
            src_ref=src,
            dst_ref=dst,
            send_sem=send,
            recv_sem=recv,
            device_id=device,
            device_id_type=MESH,
        )

    pairs = [remote(cotangent, c_pair, pair_send.at[4], pair_recv.at[4], partner)]
    pairs[0].start()
    for i, yy in enumerate(order):
        cols = pl.multiple_of(yy * 2048 + (1 - core) * 1024, 1024)
        copy = remote(
            hidden.at[:, pl.ds(cols, 1024)],
            h_pair.at[i],
            pair_send.at[i],
            pair_recv.at[i],
            partner,
        )
        copy.start()
        pairs.append(copy)

    bufs, fars, nears = (b0, b1, b2), (f0, f1, f2), (n0, n1, n2)

    class Stage:
        def __init__(self, colour, phase):
            self.axis = ORDER[colour][phase]
            self.mine = here[self.axis]
            index = tuple(here[a] for a in ORDER[colour][:phase])
            self.buf = bufs[colour].at[index] if phase else bufs[colour]
            self.phase = phase
            rows = ROWS[colour]
            if phase == 0:
                self.halves = ((pl.ds(0, 2),), (pl.ds(2, 2),))
            elif phase == 1:
                self.halves = ((pl.ds(0, 2),), (pl.ds(2, 2),))
            else:
                cut_at = SPLIT[colour]
                self.halves = ((pl.ds(0, cut_at),), (pl.ds(cut_at, rows - cut_at),))
            self.far = [fars[colour][phase].at[d] for d in range(2)]
            if phase == 2:
                self.far = [fars[colour][phase].at[d, h[0]] for d, h in enumerate(self.halves)]
            self.near = [nears[colour][phase].at[d] for d in range(2)]
            base = (colour * 3 + phase) * 6
            self.copies = []
            for d, step in enumerate((1, -1)):
                to = neighbour(self.axis, step)
                far = self.buf.at[((self.mine + 2) % 4,) + self.halves[d]]
                close = (self.mine + step) % 4
                own = self.buf.at[(close,) + self.halves[1 - d]]
                acc = self.buf.at[(close,) + self.halves[d]]
                self.copies.append(
                    (
                        remote(far, self.far[d], ring_send.at[base + d], ring_recv.at[base + d], to),
                        remote(
                            own,
                            self.near[d].at[self.halves[1 - d]],
                            ring_send.at[base + 2 + d],
                            ring_recv.at[base + 2 + d],
                            to,
                        ),
                        remote(
                            acc,
                            self.near[d].at[self.halves[d]],
                            ring_send.at[base + 4 + d],
                            ring_recv.at[base + 4 + d],
                            to,
                        ),
                        acc,
                    )
                )

        def four(self, ref):
            return ref

        def add(self, target, parts):
            if self.phase == 0:
                add_into(target, parts)
            elif self.phase == 1:
                for i in range(target.shape[0]):
                    total = target[i]
                    for part in parts:
                        total = total + part[i]
                    target[i] = total
            else:
                total = target[...]
                for part in parts:
                    total = total + part[...]
                target[...] = total

        def begin(self):
            for d in range(2):
                self.copies[d][0].start()
            for d in range(2):
                self.copies[d][1].start()

        def middle(self):
            for d in range(2):
                far, _, onward, acc = self.copies[d]
                far.wait_recv()
                self.add(acc, [self.far[d]])
                onward.start()

        def finish(self):
            for d in range(2):
                self.copies[d][1].wait_recv()
                self.copies[d][2].wait_recv()
            self.add(self.buf.at[self.mine], self.near)

        def drain(self):
            for d in range(2):
                for c in range(3):
                    self.copies[d][c].wait_send()

    loads[0].wait()
    pairs[0].wait_recv()
    for i, yy in enumerate(order):
        loads[1 + i].wait()
        pairs[1 + i].wait_recv()

        def body(zz, carry, i=i, yy=yy):
            cols = pl.ds(pl.multiple_of(zz * 256, 256), 256)
            dims = (((0,), (0,)), ((), ()))
            total = lax.dot_general(
                h_own[i, :, cols], c_own[...], dims, preferred_element_type=jnp.float32
            ) + lax.dot_general(
                h_pair[i, :, cols], c_pair[...], dims, preferred_element_type=jnp.float32
            )
            for xx in range(4):
                part = total[xx * 64 : xx * 64 + 64]
                b0[yy, zz, xx, 0:64, :] = part[:, 0:128]
                b0[yy, zz, xx, 64:88, :] = part[0:24, 128:256]
                b1[zz, xx, yy, 0:40, :] = part[24:64, 128:256]
                b1[zz, xx, yy, 40:88, :] = part[0:48, 256:384]
                b2[xx, yy, zz, 0:16, :] = part[48:64, 256:384]
                b2[xx, yy, zz, 16:80, :] = part[:, 384:512]
            return carry

        lax.fori_loop(0, 4, body, 0)

    for phase in range(3):
        stages = [Stage(colour, phase) for colour in range(3)]
        for s in stages:
            s.begin()
        for s in stages:
            s.middle()
        for s in stages:
            s.finish()
        for s in stages:
            s.drain()

    for colour in range(3):
        index = tuple(here[a] for a in ORDER[colour])
        grad[FIRST[colour] : FIRST[colour] + ROWS[colour], :] = bufs[colour][index] * (1.0 / 65536)

    g = grad[...]
    squares = jnp.sum((g * g).reshape(32, 8, 128), axis=0)

    def gather(table, mine, count, base, target):
        copies = []
        for s in range(1, count):
            copies.append(
                remote(
                    table.at[mine],
                    table.at[mine],
                    sum_send.at[base + s],
                    sum_recv.at[base + s],
                    target(s),
                )
            )
        for c in copies:
            c.start()
        for c in copies:
            c.wait()
        total = table[0]
        for s in range(1, count):
            total = total + table[s]
        return total

    plane[fs] = squares
    squares = gather(plane, fs, 16, 0, lambda s: (cut, (fs + s) % 16))
    line[cut] = squares
    squares = gather(line, cut, 8, 16, lambda s: ((cut + s) % 8, fs))
    norm = jnp.sqrt(jnp.sum(squares, keepdims=True))
    factor = jnp.minimum(1.0, clip_norm / (norm + 1e-06))

    for h in range(2):
        m_new, v_new = [], []
        for j in (2 * h, 2 * h + 1):
            cols = slice(j * 128, j * 128 + 128)
            clipped = grad[j * 64 : j * 64 + 64, :] * factor
            m_old = first[:, cols].astype(jnp.float32) * scales[:, h : h + 1]
            v_old = second[:, cols].astype(jnp.float32) * scales[:, 2 + h : 3 + h]
            m = beta_first * m_old + (1.0 - beta_first) * clipped
            v = beta_second * v_old + (1.0 - beta_second) * clipped * clipped
            m_hat = m / (1.0 - beta_first**STEP)
            v_hat = v / (1.0 - beta_second**STEP)
            w_old = weight[:, cols].astype(jnp.float32)
            w_out[:, cols] = (
                w_old
                - learn_rate * (m_hat / (jnp.sqrt(v_hat) + adam_epsilon) + weight_decay * w_old)
            ).astype(jnp.bfloat16)
            m_new.append(m)
            v_new.append(v)
        m_scale = (
            jnp.max(jnp.maximum(jnp.abs(m_new[0]), jnp.abs(m_new[1])), axis=1, keepdims=True)
            + tiny_scale
        )
        v_scale = jnp.max(jnp.maximum(v_new[0], v_new[1]), axis=1, keepdims=True) + tiny_scale
        ms_out[:, h : h + 1] = m_scale
        vs_out[:, h : h + 1] = v_scale
        for n, j in enumerate((2 * h, 2 * h + 1)):
            cols = slice(j * 128, j * 128 + 128)
            m_out[:, cols] = (m_new[n] / m_scale).astype(jnp.bfloat16)
            v_out[:, cols] = (v_new[n] / v_scale).astype(jnp.bfloat16)

    for c in pairs:
        c.wait_send()


def main_call(hidden, cotangent, weight, first, second, scales):
    vmem = pl.BlockSpec(memory_space=pltpu.VMEM)
    hbm = pl.BlockSpec(memory_space=pl.ANY)
    f32, b16 = jnp.float32, jnp.bfloat16
    scratch = [
        pltpu.VMEM((4, 512, 1024), b16),
        pltpu.VMEM((4, 512, 1024), b16),
        pltpu.VMEM((512, 512), b16),
        pltpu.VMEM((512, 512), b16),
    ]
    scratch += [pltpu.VMEM((4, 4, 4, r, 128), f32) for r in ROWS]
    scratch += [
        [
            pltpu.VMEM((2, 2, 4, r, 128), f32),
            pltpu.VMEM((2, 2, r, 128), f32),
            pltpu.VMEM((2, r, 128), f32),
        ]
        for r in ROWS
    ]
    scratch += [
        [
            pltpu.VMEM((2, 4, 4, r, 128), f32),
            pltpu.VMEM((2, 4, r, 128), f32),
            pltpu.VMEM((2, r, 128), f32),
        ]
        for r in ROWS
    ]
    scratch += [
        pltpu.VMEM((256, 128), f32),
        pltpu.VMEM((16, 8, 128), f32),
        pltpu.VMEM((8, 8, 128), f32),
        pltpu.SemaphoreType.DMA((5,)),
        pltpu.SemaphoreType.DMA((5,)),
        pltpu.SemaphoreType.DMA((5,)),
        pltpu.SemaphoreType.DMA((54,)),
        pltpu.SemaphoreType.DMA((54,)),
        pltpu.SemaphoreType.DMA((24,)),
        pltpu.SemaphoreType.DMA((24,)),
    ]
    return pl.pallas_call(
        main_kernel,
        out_shape=(
            jax.ShapeDtypeStruct((64, 512), b16),
            jax.ShapeDtypeStruct((64, 512), b16),
            jax.ShapeDtypeStruct((64, 2), f32),
            jax.ShapeDtypeStruct((64, 512), b16),
            jax.ShapeDtypeStruct((64, 2), f32),
        ),
        in_specs=[hbm, hbm, vmem, vmem, vmem, vmem],
        out_specs=(vmem,) * 5,
        scratch_shapes=scratch,
        compiler_params=pltpu.CompilerParams(
            collective_id=0, has_side_effects=True, vmem_limit_bytes=60 * 1024 * 1024
        ),
        name="gradient_adam",
    )(hidden, cotangent, weight, first, second, scales)


def three_parts(values):
    high = lax.reduce_precision(values, 8, 7)
    rest = values - high
    middle = lax.reduce_precision(rest, 8, 7)
    return [part.astype(jnp.bfloat16) for part in (high, middle, rest - middle)]


def shards(
    hidden_states,
    key_cotangent,
    old_weight,
    old_first,
    old_first_scale,
    old_second,
    old_second_scale,
    send_counts,
):
    f32, b16 = jnp.float32, jnp.bfloat16
    counts = send_counts[0]
    index = jnp.arange(128, dtype=jnp.int32)
    starts = jnp.sum(jnp.where(index[None, :] < index[:, None], counts[None, :], 0), axis=1)
    lane = jnp.arange(2, dtype=jnp.int32)
    live = lane[None, :] < counts[:, None]
    slot = starts[:, None] + lane[None, :]
    pick = (live[:, :, None] & (slot[:, :, None] == index[None, None, :])).astype(b16)
    side = jnp.stack(
        three_parts(old_first_scale)
        + three_parts(old_second_scale)
        + [jnp.ones((128,), b16)]
        + [jnp.zeros((128,), b16)] * 121,
        axis=1,
    )
    stacked = jnp.concatenate([old_weight, old_first, old_second, side], axis=1)
    packed = lax.dot_general(
        pick.reshape(256, 128), stacked, (((1,), (0,)), ((), ())), preferred_element_type=f32
    ).astype(b16)
    arrived = lax.all_to_all(
        packed.reshape(128, 2, 896), AXES, split_axis=0, concat_axis=0, tiled=True
    ).reshape(256, 896)
    here = arrived[:, 774] > 0.5
    count = here.astype(jnp.int32)
    wide = jnp.arange(256, dtype=jnp.int32)
    target = jnp.sum(jnp.where(wide[None, :] < wide[:, None], count[None, :], 0), axis=1)
    rows = jnp.arange(64, dtype=jnp.int32)
    owned = []
    for h in range(2):
        choose = (here[None, :] & (target[None, :] == 2 * rows[:, None] + h)).astype(b16)
        owned.append(
            lax.dot_general(
                choose, arrived, (((1,), (0,)), ((), ())), preferred_element_type=f32
            )
        )
    weight, first, second = (
        jnp.concatenate([o[:, a * 256 : a * 256 + 256] for o in owned], axis=1).astype(b16)
        for a in range(3)
    )
    scales = jnp.stack(
        [o[:, c] + o[:, c + 1] + o[:, c + 2] for c in (768, 771) for o in owned], axis=1
    )
    gathered = lax.all_gather(weight, AXES, axis=0, tiled=True)
    w_new, m_code, m_scale, v_code, v_scale = main_call(
        hidden_states, key_cotangent, weight, first, second, scales
    )
    input_grad = lax.dot_general(
        key_cotangent, gathered, (((1,), (1,)), ((), ())), preferred_element_type=f32
    ).astype(b16)
    return (input_grad, w_new, m_code, m_scale, v_code, v_scale)


def solution(mesh):
    rows = P(AXES, None)
    placed = (rows, rows, rows, rows, P(AXES), rows, P(AXES), rows)
    return jax.shard_map(
        shards, mesh=mesh, in_specs=placed, out_specs=(rows,) * 6, check_vma=False
    )
```

```python
import jax
import jax.numpy as jnp
from jax import lax
from jax.experimental import pallas as pl
from jax.experimental.pallas import tpu as pltpu
from jax.sharding import PartitionSpec as P

STEP = 2000

beta_first = 0.9
beta_second = 0.95
adam_epsilon = 1e-05
learn_rate = 0.001
weight_decay = 0.1
clip_norm = 1.0
tiny_scale = 1e-30

ROWS_OUT = (((0,), (0,)), ((), ()))
AXES = ("cuts", "fsdp")
MESH = pl.DeviceIdType.MESH
ROWS = (88, 88, 80)
FIRST = (0, 88, 176)
ORDER = ((0, 1, 2), (1, 2, 0), (2, 0, 1))
SPLIT = (48, 48, 40)
W_ROWS = (24, 24, 16)
W_FIRST = (0, 24, 48)


def add_into(target, parts):
    outer, inner = target.shape[:2]

    def body(i, carry):
        a, b = i // inner, i % inner
        total = target[a, b]
        for part in parts:
            total = total + part[a, b]
        target[a, b] = total
        return carry

    lax.fori_loop(0, outer * inner, body, 0)


def main_kernel(
    hidden,
    cotangent,
    weight_in,
    first_in,
    second_in,
    first_by_in,
    second_by_in,
    counts_in,
    whole,
    c_own,
    w_out,
    m_out,
    ms_out,
    v_out,
    vs_out,
    h_own,
    h_pair,
    c_pair,
    b0,
    b1,
    b2,
    f0,
    f1,
    f2,
    n0,
    n1,
    n2,
    grad,
    plane,
    line,
    table,
    packed,
    middle,
    arrived,
    owned,
    weight,
    first,
    second,
    first_by,
    second_by,
    counts,
    load_sem,
    pair_send,
    pair_recv,
    ring_send,
    ring_recv,
    sum_send,
    sum_recv,
    deal_send,
    deal_recv,
    line_send,
    line_recv,
    turn_send,
    turn_recv,
    pass_send,
    pass_recv,
):
    cut = lax.axis_index("cuts")
    fs = lax.axis_index("fsdp")
    y, core = cut // 2, cut % 2
    z, x = fs // 4, fs % 4
    here = (y, z, x)

    def at(y, z, x, core):
        return (y * 2 + core, z * 4 + x)

    def neighbour(axis, step):
        place = list(here)
        place[axis] = (place[axis] + step) % 4
        return at(*place, core)

    partner = at(y, z, x, 1 - core)

    order = [(y + s) % 4 for s in (2, 1, 3, 0)]
    state = [
        pltpu.make_async_copy(a, b, load_sem.at[5 + n])
        for n, (a, b) in enumerate(
            (
                (weight_in, weight),
                (first_in, first),
                (second_in, second),
                (first_by_in, first_by),
                (second_by_in, second_by),
                (counts_in, counts),
            )
        )
    ]
    for copy in state:
        copy.start()
    loads = [pltpu.make_async_copy(cotangent, c_own, load_sem.at[4])]
    loads[0].start()
    for i, yy in enumerate(order):
        cols = pl.multiple_of(yy * 2048 + core * 1024, 1024)
        copy = pltpu.make_async_copy(hidden.at[:, pl.ds(cols, 1024)], h_own.at[i], load_sem.at[i])
        copy.start()
        loads.append(copy)

    f32, b16 = jnp.float32, jnp.bfloat16
    barrier = pltpu.get_barrier_semaphore()

    for s in range(1, 16):
        pl.semaphore_signal(barrier, inc=1, device_id=(cut, (fs + s) % 16), device_id_type=MESH)
    for s in range(1, 8):
        pl.semaphore_signal(barrier, inc=1, device_id=((cut + s) % 8, fs), device_id_type=MESH)

    row = lax.broadcasted_iota(jnp.int32, (128, 128), 0)
    col = lax.broadcasted_iota(jnp.int32, (128, 128), 1)
    for copy in state:
        copy.wait()
    mine = counts[...]
    starts = jnp.sum(jnp.where(col < row, mine, 0).astype(f32), axis=1, keepdims=True)
    amount = jnp.sum(jnp.where(col == row, mine, 0).astype(f32), axis=1, keepdims=True)
    slot = col.astype(f32)
    values = jnp.concatenate([weight[...], first[...], second[...]], axis=1)
    table[...] = jnp.zeros_like(table)
    for place in range(2):
        pick = (slot == starts + place) & (amount > place)
        chosen = jnp.dot(
            jnp.where(pick, 1.0, 0.0).astype(b16), values, preferred_element_type=f32
        )
        for q in range(6):
            table[pl.ds(place * 8 + q, 128, stride=16), :] = chosen[:, q * 128 : q * 128 + 128]
        side = jnp.where((col == 6) & (amount > place), 1.0, 0.0)
        for n, by in enumerate((first_by, second_by)):
            rest = jnp.sum(jnp.where(pick, by[...], 0.0), axis=1, keepdims=True)
            for part in range(3):
                high = rest.astype(b16).astype(f32)
                side = side + jnp.where(col == n * 3 + part, high, 0.0)
                rest = rest - high
        table[pl.ds(place * 8 + 6, 128, stride=16), :] = side
    packed[...] = table[...].astype(b16).reshape(8, 16, 16, 128)
    middle[:, fs] = packed[:, fs]

    def own_part(i):
        loads[1 + i].wait()
        spread(i, lax.dot_general(h_own[i], c_own[...], ROWS_OUT, preferred_element_type=f32), False)

    def pair_part(i):
        pairs[1 + i].wait_recv()
        spread(i, lax.dot_general(h_pair[i], c_pair[...], ROWS_OUT, preferred_element_type=f32), True)

    def spread(i, total, more):
        yy = order[i]
        for zz in range(4):
            for xx in range(4):
                part = total[zz * 256 + xx * 64 : zz * 256 + xx * 64 + 64]
                for buf, place, low, value in (
                    (b0, (yy, zz, xx), 0, part[:, 0:128]),
                    (b0, (yy, zz, xx), 64, part[0:24, 128:256]),
                    (b1, (zz, xx, yy), 0, part[24:64, 128:256]),
                    (b1, (zz, xx, yy), 40, part[0:48, 256:384]),
                    (b2, (xx, yy, zz), 0, part[48:64, 256:384]),
                    (b2, (xx, yy, zz), 16, part[:, 384:512]),
                ):
                    at = place + (slice(low, low + value.shape[0]),)
                    buf[at] = buf[at] + value if more else value

    loads[0].wait()
    own_part(0)
    own_part(1)
    pl.semaphore_wait(barrier, 22)

    def remote(src, dst, send, recv, device):
        return pltpu.make_async_remote_copy(
            src_ref=src,
            dst_ref=dst,
            send_sem=send,
            recv_sem=recv,
            device_id=device,
            device_id_type=MESH,
        )

    for s in range(1, 16):
        other = (fs + s) % 16
        remote(
            packed.at[:, other], middle.at[:, fs], deal_send, deal_recv, (cut, other)
        ).start()
    dealt = remote(
        packed.at[:, pl.ds(0, 15)], middle.at[:, pl.ds(0, 15)], deal_send, deal_recv, partner
    )

    pairs = [remote(cotangent, c_pair, pair_send.at[4], pair_recv.at[4], partner)]
    pairs[0].start()
    for i, yy in enumerate(order):
        cols = pl.multiple_of(yy * 2048 + (1 - core) * 1024, 1024)
        copy = remote(
            hidden.at[:, pl.ds(cols, 1024)],
            h_pair.at[i],
            pair_send.at[i],
            pair_recv.at[i],
            partner,
        )
        copy.start()
        pairs.append(copy)

    bufs, fars, nears = (b0, b1, b2), (f0, f1, f2), (n0, n1, n2)

    class Stage:
        def __init__(self, colour, phase):
            self.axis = ORDER[colour][phase]
            self.mine = here[self.axis]
            index = tuple(here[a] for a in ORDER[colour][:phase])
            self.buf = bufs[colour].at[index] if phase else bufs[colour]
            self.phase = phase
            rows = ROWS[colour]
            if phase == 0:
                self.halves = ((pl.ds(0, 2),), (pl.ds(2, 2),))
            elif phase == 1:
                self.halves = ((pl.ds(0, 2),), (pl.ds(2, 2),))
            else:
                cut_at = SPLIT[colour]
                self.halves = ((pl.ds(0, cut_at),), (pl.ds(cut_at, rows - cut_at),))
            self.far = [fars[colour][phase].at[d] for d in range(2)]
            if phase == 2:
                self.far = [fars[colour][phase].at[d, h[0]] for d, h in enumerate(self.halves)]
            self.near = [nears[colour][phase].at[d] for d in range(2)]
            base = (colour * 3 + phase) * 6
            self.copies = []
            for d, step in enumerate((1, -1)):
                to = neighbour(self.axis, step)
                far = self.buf.at[((self.mine + 2) % 4,) + self.halves[d]]
                close = (self.mine + step) % 4
                own = self.buf.at[(close,) + self.halves[1 - d]]
                acc = self.buf.at[(close,) + self.halves[d]]
                self.copies.append(
                    (
                        remote(far, self.far[d], ring_send.at[base + d], ring_recv.at[base + d], to),
                        remote(
                            own,
                            self.near[d].at[self.halves[1 - d]],
                            ring_send.at[base + 2 + d],
                            ring_recv.at[base + 2 + d],
                            to,
                        ),
                        remote(
                            acc,
                            self.near[d].at[self.halves[d]],
                            ring_send.at[base + 4 + d],
                            ring_recv.at[base + 4 + d],
                            to,
                        ),
                        acc,
                    )
                )

        def add(self, target, parts):
            if self.phase == 0:
                add_into(target, parts)
            elif self.phase == 1:
                for i in range(target.shape[0]):
                    total = target[i]
                    for part in parts:
                        total = total + part[i]
                    target[i] = total
            else:
                total = target[...]
                for part in parts:
                    total = total + part[...]
                target[...] = total

        def far_out(self):
            for d in range(2):
                self.copies[d][0].start()

        def own_out(self):
            for d in range(2):
                self.copies[d][1].start()

        def middle(self):
            for d in range(2):
                far, _, onward, acc = self.copies[d]
                far.wait_recv()
                self.add(acc, [self.far[d]])
                onward.start()

        def finish(self):
            for d in range(2):
                self.copies[d][1].wait_recv()
                self.copies[d][2].wait_recv()
            self.add(self.buf.at[self.mine], self.near)

        def drain(self):
            for d in range(2):
                for c in range(3):
                    self.copies[d][c].wait_send()

    class Turn:
        def __init__(self, colour, phase):
            self.colour, self.phase = colour, phase
            self.axis = ORDER[colour][phase]
            self.mine = here[self.axis]
            pieces = range(4) if phase == 2 else (None,)
            base = (0, 12, 24)[phase] + colour * (12 if phase == 2 else 4)
            self.begun, self.onward = ([], []), ([], [])
            for d, step in enumerate((1, -1)):
                to = neighbour(self.axis, step)
                for piece in pieces if d == 0 or phase < 2 else (2, 3, 0, 1):
                    own = self.region(self.mine, piece=piece)
                    self.begun[d].append(
                        remote(own, own, turn_send.at[base], turn_recv.at[base], to)
                    )
                    base += 1
                for piece in ((0, 1), (2, 3))[d] if phase == 2 else (None,):
                    other = self.region((self.mine - step) % 4, d if phase < 2 else None, piece)
                    self.onward[d].append(
                        remote(other, other, turn_send.at[base], turn_recv.at[base], to)
                    )
                    base += 1

        def region(self, index, half=None, piece=None):
            place = list(here)
            for a in ORDER[self.colour][: self.phase]:
                place[a] = pl.ds(0, 4)
            place[self.axis] = index
            cols = pl.ds(0, 512)
            if half is not None and self.phase == 0:
                cols = pl.ds(half * 256, 256)
            elif half is not None:
                place[ORDER[self.colour][0]] = pl.ds(half * 2, 2)
            if piece is not None:
                place[ORDER[self.colour][0]] = piece
            rows = pl.ds(W_FIRST[self.colour], W_ROWS[self.colour])
            return whole.at[place[0], core, place[1], place[2], rows, cols]

        def begin(self, n=0):
            for d in range(2):
                self.begun[d][n].start()

        def middle(self, n=0):
            for d in range(2):
                self.begun[d][n].wait_recv()
                self.onward[d][n].start()

        def arrive(self, n):
            for d in range(2):
                self.begun[d][n].wait_recv()

        def finish(self, n=0):
            for d in range(2):
                self.onward[d][n].wait_recv()

        def drain(self):
            for d in range(2):
                for c in self.begun[d] + self.onward[d]:
                    c.wait_send()

    def hand(turn, index, n):
        slab = turn.region(index)
        k = turn.colour * 4 + n
        return remote(slab, slab, pass_send.at[k], pass_recv.at[k], partner)

    stages = [[Stage(colour, phase) for colour in range(3)] for phase in range(3)]
    turns = [[Turn(colour, phase) for colour in range(3)] for phase in range(3)]

    def each(things, step, *given):
        for thing in things:
            getattr(thing, step)(*given)

    def unpack():
        lined.wait_recv()
        table[...] = arrived[...].reshape(2048, 128).astype(f32)
        marks, before = [], 0.0
        for place in range(2):
            mark = table[pl.ds(place * 8 + 6, 128, stride=16), :][:, 6:7]
            marks.append(jnp.sum(jnp.where(row == col, mark, 0.0), axis=0, keepdims=True))
            before = before + jnp.sum(jnp.where(row < col, mark, 0.0), axis=0, keepdims=True)
        target = jnp.concatenate([before, before + marks[0]], axis=1)
        mark = jnp.concatenate(marks, axis=1)
        blocks = jnp.concatenate(
            [
                jnp.concatenate(
                    [table[pl.ds(place * 8 + q, 128, stride=16), :].astype(b16) for q in range(7)],
                    axis=1,
                )
                for place in range(2)
            ],
            axis=0,
        )
        new_row = lax.broadcasted_iota(jnp.int32, (64, 256), 0).astype(f32)
        for h in range(2):
            choose = (target == 2.0 * new_row + h) & (mark > 0.5)
            owned[h] = jnp.dot(
                jnp.where(choose, 1.0, 0.0).astype(b16), blocks, preferred_element_type=f32
            )
            whole[y, core, z, x, :, h * 256 : h * 256 + 256] = owned[h, :, 0:256].astype(b16)


    own_part(2)
    own_part(3)
    dealt.wait_recv()
    arrived[cut] = middle[cut]
    for s in range(1, 8):
        other = (cut + s) % 8
        remote(middle.at[other], arrived.at[cut], line_send, line_recv, (other, fs)).start()
    lined = remote(
        middle.at[pl.ds(0, 7)], arrived.at[pl.ds(0, 7)], line_send, line_recv, partner
    )
    pairs[0].wait_recv()
    pair_part(0)
    each(stages[0][:1], "far_out")
    pair_part(1)
    pair_part(2)
    pair_part(3)
    each(stages[0][1:], "far_out")
    unpack()
    each(turns[0], "begin")
    each(stages[0], "own_out")
    each(turns[0], "middle")
    each(stages[0], "middle")
    each(turns[0], "finish")
    each(turns[1], "begin")
    each(stages[0], "finish")
    each(stages[1], "far_out")
    each(stages[1], "own_out")
    each(turns[1], "middle")
    each(stages[1], "middle")
    each(turns[1], "finish")
    each(turns[2], "begin", 0)
    passes = [hand(t, t.mine, 0) for t in turns[2]]
    for p in passes:
        p.start()
    each(stages[1], "finish")
    each(stages[2], "far_out")
    each(stages[2], "own_out")
    each(turns[2], "begin", 1)
    each(turns[2], "middle", 0)
    each(stages[2], "middle")
    each(turns[2], "begin", 2)
    each(stages[2], "finish")

    for colour in range(3):
        index = tuple(here[a] for a in ORDER[colour])
        grad[FIRST[colour] : FIRST[colour] + ROWS[colour], :] = bufs[colour][index] * (1.0 / 65536)

    g = grad[...]
    squares = jnp.sum((g * g).reshape(32, 8, 128), axis=0)

    def tell(board, mine, count, base, target):
        copies = [
            remote(
                board.at[mine], board.at[mine], sum_send.at[base + s], sum_recv.at[base + s], target(s)
            )
            for s in range(1, count)
        ]
        for c in copies:
            c.start()
        return copies

    def hear(board, count, copies):
        for c in copies:
            c.wait()
        total = board[0]
        for s in range(1, count):
            total = total + board[s]
        return total

    plane[fs] = squares
    told = tell(plane, fs, 16, 0, lambda s: (cut, (fs + s) % 16))
    each(turns[2], "begin", 3)
    each(turns[2], "middle", 1)
    for t in turns[2]:
        t.arrive(2)
        t.arrive(3)
        for n, step in ((1, -1), (2, 1)):
            p = hand(t, (t.mine + step) % 4, n)
            p.start()
            passes.append(p)
    squares = hear(plane, 16, told)
    line[cut] = squares
    told = tell(line, cut, 8, 16, lambda s: ((cut + s) % 8, fs))
    for t in turns[2]:
        t.finish(0)
        t.finish(1)
        p = hand(t, (t.mine + 2) % 4, 3)
        p.start()
        passes.append(p)
    squares = hear(line, 8, told)
    norm = jnp.sqrt(jnp.sum(squares, keepdims=True))
    factor = jnp.minimum(1.0, clip_norm / (norm + 1e-06))

    eye = lax.broadcasted_iota(jnp.int32, (64, 64), 0) == lax.broadcasted_iota(
        jnp.int32, (64, 64), 1
    )
    for h in range(2):
        m_new, v_new = [], []
        m_by = owned[h, :, 768:769] + owned[h, :, 769:770] + owned[h, :, 770:771]
        v_by = owned[h, :, 771:772] + owned[h, :, 772:773] + owned[h, :, 773:774]
        for n in range(2):
            j = 2 * h + n
            cols = slice(j * 128, j * 128 + 128)
            clipped = grad[j * 64 : j * 64 + 64, :] * factor
            m_old = owned[h, :, 256 + n * 128 : 384 + n * 128] * m_by
            v_old = owned[h, :, 512 + n * 128 : 640 + n * 128] * v_by
            m = beta_first * m_old + (1.0 - beta_first) * clipped
            v = beta_second * v_old + (1.0 - beta_second) * clipped * clipped
            m_hat = m / (1.0 - beta_first**STEP)
            v_hat = v / (1.0 - beta_second**STEP)
            w_old = owned[h, :, n * 128 : n * 128 + 128]
            w_out[:, cols] = (
                w_old
                - learn_rate * (m_hat / (jnp.sqrt(v_hat) + adam_epsilon) + weight_decay * w_old)
            ).astype(b16)
            m_new.append(m)
            v_new.append(v)
        m_scale = (
            jnp.max(jnp.maximum(jnp.abs(m_new[0]), jnp.abs(m_new[1])), axis=1, keepdims=True)
            + tiny_scale
        )
        v_scale = jnp.max(jnp.maximum(v_new[0], v_new[1]), axis=1, keepdims=True) + tiny_scale
        ms_out[h : h + 1, :] = jnp.sum(jnp.where(eye, m_scale, 0.0), axis=0, keepdims=True)
        vs_out[h : h + 1, :] = jnp.sum(jnp.where(eye, v_scale, 0.0), axis=0, keepdims=True)
        for n in range(2):
            cols = slice((2 * h + n) * 128, (2 * h + n) * 128 + 128)
            m_out[:, cols] = (m_new[n] / m_scale).astype(b16)
            v_out[:, cols] = (v_new[n] / v_scale).astype(b16)

    for p in passes:
        p.wait()
    for c in pairs:
        c.wait_send()
    lined.wait_send()
    dealt.wait_send()
    for group in stages + turns:
        each(group, "drain")


def main_call(*given):
    vmem = pl.BlockSpec(memory_space=pltpu.VMEM)
    hbm = pl.BlockSpec(memory_space=pltpu.HBM)
    f32, b16 = jnp.float32, jnp.bfloat16
    scratch = [
        pltpu.VMEM((4, 512, 1024), b16),
        pltpu.VMEM((4, 512, 1024), b16),
        pltpu.VMEM((512, 512), b16),
    ]
    scratch += [pltpu.VMEM((4, 4, 4, r, 128), f32) for r in ROWS]
    scratch += [
        [
            pltpu.VMEM((2, 2, 4, r, 128), f32),
            pltpu.VMEM((2, 2, r, 128), f32),
            pltpu.VMEM((2, r, 128), f32),
        ]
        for r in ROWS
    ]
    scratch += [
        [
            pltpu.VMEM((2, 4, 4, r, 128), f32),
            pltpu.VMEM((2, 4, r, 128), f32),
            pltpu.VMEM((2, r, 128), f32),
        ]
        for r in ROWS
    ]
    scratch += [
        pltpu.VMEM((256, 128), f32),
        pltpu.VMEM((16, 8, 128), f32),
        pltpu.VMEM((8, 8, 128), f32),
        pltpu.VMEM((2048, 128), f32),
        pltpu.VMEM((8, 16, 16, 128), b16),
        pltpu.VMEM((8, 16, 16, 128), b16),
        pltpu.VMEM((8, 16, 16, 128), b16),
        pltpu.VMEM((2, 64, 896), f32),
        pltpu.VMEM((128, 256), b16),
        pltpu.VMEM((128, 256), b16),
        pltpu.VMEM((128, 256), b16),
        pltpu.VMEM((1, 128), f32),
        pltpu.VMEM((1, 128), f32),
        pltpu.VMEM((1, 128), jnp.int32),
        pltpu.SemaphoreType.DMA((11,)),
        pltpu.SemaphoreType.DMA((5,)),
        pltpu.SemaphoreType.DMA((5,)),
        pltpu.SemaphoreType.DMA((54,)),
        pltpu.SemaphoreType.DMA((54,)),
        pltpu.SemaphoreType.DMA((24,)),
        pltpu.SemaphoreType.DMA((24,)),
        pltpu.SemaphoreType.DMA,
        pltpu.SemaphoreType.DMA,
        pltpu.SemaphoreType.DMA,
        pltpu.SemaphoreType.DMA,
        pltpu.SemaphoreType.DMA((60,)),
        pltpu.SemaphoreType.DMA((60,)),
        pltpu.SemaphoreType.DMA((12,)),
        pltpu.SemaphoreType.DMA((12,)),
    ]
    return pl.pallas_call(
        main_kernel,
        out_shape=(
            pltpu.VMEM((4, 2, 4, 4, 64, 512), b16),
            pltpu.VMEM((512, 512), b16),
            pltpu.VMEM((64, 512), b16),
            pltpu.VMEM((64, 512), b16),
            pltpu.VMEM((2, 64), f32),
            pltpu.VMEM((64, 512), b16),
            pltpu.VMEM((2, 64), f32),
        ),
        in_specs=[hbm] * 8,
        out_specs=(vmem,) * 7,
        scratch_shapes=scratch,
        compiler_params=pltpu.CompilerParams(
            collective_id=0, has_side_effects=True, vmem_limit_bytes=57_400_000
        ),
        name="exchange_adam",
    )(*given)


def last_kernel(cotangent, weight, *refs):
    given, (out, *kept), (slab, sems) = refs[:5], refs[5:11], refs[11:]
    copies = []
    for y in range(4):
        for core in range(2):
            i = y * 2 + core
            slab[i] = lax.dot_general(
                cotangent[...],
                weight[y, core].reshape(1024, 512),
                (((1,), (1,)), ((), ())),
                preferred_element_type=jnp.float32,
            ).astype(jnp.bfloat16)
            copies.append(
                pltpu.make_async_copy(
                    slab.at[i], out.at[:, pl.ds(i * 1024, 1024)], sems.at[i]
                )
            )
            copies[-1].start()
    for a, b in zip(given, kept):
        b[...] = a[...]
    for c in copies:
        c.wait()


def last_call(cotangent, weight, small):
    vmem = pl.BlockSpec(memory_space=pltpu.VMEM)
    held = [pltpu.with_memory_space_constraint(a, pltpu.VMEM) for a in (cotangent, weight, *small)]
    return pl.pallas_call(
        last_kernel,
        out_shape=[jax.ShapeDtypeStruct((512, 8192), jnp.bfloat16)]
        + [jax.ShapeDtypeStruct(a.shape, a.dtype) for a in small],
        in_specs=[vmem] * 7,
        out_specs=[pl.BlockSpec(memory_space=pl.ANY)] + [vmem] * 5,
        scratch_shapes=[pltpu.VMEM((8, 512, 1024), jnp.bfloat16), pltpu.SemaphoreType.DMA((8,))],
        compiler_params=pltpu.CompilerParams(vmem_limit_bytes=24_000_000),
        name="input_grad",
    )(*held)


def shards(
    hidden_states,
    key_cotangent,
    old_weight,
    old_first,
    old_first_scale,
    old_second,
    old_second_scale,
    send_counts,
):
    gathered, cotangent, *small = main_call(
        hidden_states, key_cotangent, old_weight, old_first, old_second,
        old_first_scale[None], old_second_scale[None], send_counts,
    )
    input_grad, w_new, m_code, m_scale, v_code, v_scale = last_call(
        cotangent, gathered, small
    )
    return (input_grad, w_new, m_code, m_scale.T, v_code, v_scale.T)


def solution(mesh):
    rows = P(AXES, None)
    placed = (rows, rows, rows, rows, P(AXES), rows, P(AXES), rows)
    return jax.shard_map(
        shards, mesh=mesh, in_specs=placed, out_specs=(rows,) * 6, check_vma=False
    )
```

```python
import jax
import jax.numpy as jnp
from jax import lax
from jax.experimental import pallas as pl
from jax.experimental.pallas import tpu as pltpu
from jax.sharding import PartitionSpec as P

STEP = 2000

beta_first = 0.9
beta_second = 0.95
adam_epsilon = 1e-05
learn_rate = 0.001
weight_decay = 0.1
clip_norm = 1.0
tiny_scale = 1e-30

ROWS_OUT = (((0,), (0,)), ((), ()))
AXES = ("cuts", "fsdp")
MESH = pl.DeviceIdType.MESH
ROWS = (88, 88, 80)
FIRST = (0, 88, 176)
ORDER = ((0, 1, 2), (1, 2, 0), (2, 0, 1))
SPLIT = (48, 48, 40)
W_ROWS = (24, 24, 16)
W_FIRST = (0, 24, 48)


def add_into(target, parts):
    outer, inner = target.shape[:2]

    def body(i, carry):
        a, b = i // inner, i % inner
        total = target[a, b]
        for part in parts:
            total = total + part[a, b]
        target[a, b] = total
        return carry

    lax.fori_loop(0, outer * inner, body, 0)


def main_kernel(
    hidden,
    cotangent,
    weight_in,
    first_in,
    second_in,
    first_by_in,
    second_by_in,
    counts_in,
    whole,
    c_own,
    w_out,
    m_out,
    ms_out,
    v_out,
    vs_out,
    h_own,
    h_pair,
    c_pair,
    b0,
    b1,
    b2,
    f0,
    f1,
    f2,
    n0,
    n1,
    n2,
    grad,
    plane,
    line,
    table,
    packed,
    middle,
    arrived,
    second_out,
    second_mid,
    second_last,
    owned,
    weight,
    first,
    second,
    first_by,
    second_by,
    counts,
    load_sem,
    pair_send,
    pair_recv,
    ring_send,
    ring_recv,
    far_send,
    far_recv,
    sum_send,
    sum_recv,
    deal_send,
    deal_recv,
    line_send,
    line_recv,
    extra_send,
    extra_recv,
    extra_line_send,
    extra_line_recv,
    turn_send,
    turn_recv,
    pass_send,
    pass_recv,
):
    cut = lax.axis_index("cuts")
    fs = lax.axis_index("fsdp")
    y, core = cut // 2, cut % 2
    z, x = fs // 4, fs % 4
    here = (y, z, x)

    def at(y, z, x, core):
        return (y * 2 + core, z * 4 + x)

    def neighbour(axis, step):
        place = list(here)
        place[axis] = (place[axis] + step) % 4
        return at(*place, core)

    partner = at(y, z, x, 1 - core)

    order = [(y + s) % 4 for s in (2, 1, 3, 0)]
    state = [
        pltpu.make_async_copy(a, b, load_sem.at[5 + n])
        for n, (a, b) in enumerate(
            (
                (weight_in, weight),
                (first_in, first),
                (second_in, second),
                (first_by_in, first_by),
                (second_by_in, second_by),
                (counts_in, counts),
            )
        )
    ]
    for copy in state:
        copy.start()
    loads = [pltpu.make_async_copy(cotangent, c_own, load_sem.at[4])]
    loads[0].start()
    for i, yy in enumerate(order):
        cols = pl.multiple_of(yy * 2048 + core * 1024, 1024)
        copy = pltpu.make_async_copy(hidden.at[:, pl.ds(cols, 1024)], h_own.at[i], load_sem.at[i])
        copy.start()
        loads.append(copy)

    f32, b16 = jnp.float32, jnp.bfloat16
    barrier = pltpu.get_barrier_semaphore()

    for s in range(1, 16):
        pl.semaphore_signal(barrier, inc=1, device_id=(cut, (fs + s) % 16), device_id_type=MESH)
    for s in range(1, 8):
        pl.semaphore_signal(barrier, inc=1, device_id=((cut + s) % 8, fs), device_id_type=MESH)

    row = lax.broadcasted_iota(jnp.int32, (128, 128), 0)
    col = lax.broadcasted_iota(jnp.int32, (128, 128), 1)
    for copy in state:
        copy.wait()
    mine = counts[...]
    starts = jnp.sum(jnp.where(col < row, mine, 0).astype(f32), axis=1, keepdims=True)
    amount = jnp.sum(jnp.where(col == row, mine, 0).astype(f32), axis=1, keepdims=True)
    slot = col.astype(f32)
    values = jnp.concatenate([weight[...], first[...], second[...]], axis=1)
    table[...] = jnp.zeros_like(table)

    def sided(pick, rows, seven):
        side = jnp.where(rows == 6, 1.0, 0.0) * jnp.sum(pick, axis=1, keepdims=True)
        side = side + jnp.where(rows == 7, seven, 0.0)
        for n, by in enumerate((first_by, second_by)):
            rest = jnp.sum(pick * by[...], axis=1, keepdims=True)
            for part in range(3):
                high = rest.astype(b16).astype(f32)
                side = side + jnp.where(rows == n * 3 + part, high, 0.0)
                rest = rest - high
        return side

    pick = jnp.where((slot == starts) & (amount > 0), 1.0, 0.0)
    chosen = jnp.dot(pick.astype(b16), values, preferred_element_type=f32)
    for q in range(6):
        table[pl.ds(q, 128, stride=8), :] = chosen[:, q * 128 : q * 128 + 128]
    table[pl.ds(6, 128, stride=8), :] = sided(pick, col, amount)
    packed[...] = table[...].astype(b16).reshape(8, 16, 8, 128)
    middle[:, fs] = packed[:, fs]
    twice = amount > 1
    pick = jnp.sum(jnp.where(twice & (slot == starts + 1), 1.0, 0.0), axis=0, keepdims=True)
    owner = jnp.sum(
        jnp.where(twice, row[:, 0:1].astype(f32), 0.0), axis=0, keepdims=True
    )
    pick = jnp.broadcast_to(pick, (8, 128))
    chosen = jnp.dot(pick.astype(b16), values, preferred_element_type=f32)
    eight = row[0:8]
    extra = jnp.where(eight == 6, sided(pick, col[0:8], owner), 0.0)
    for q in range(6):
        extra = extra + jnp.where(eight == q, chosen[:, q * 128 : q * 128 + 128], 0.0)
    second_out[fs] = extra.astype(b16)

    def own_part(i):
        loads[1 + i].wait()
        spread(i, lax.dot_general(h_own[i], c_own[...], ROWS_OUT, preferred_element_type=f32), False)

    def pair_part(i):
        pairs[1 + i].wait_recv()
        spread(i, lax.dot_general(h_pair[i], c_pair[...], ROWS_OUT, preferred_element_type=f32), True)

    def spread(i, total, more):
        yy = order[i]
        for zz in range(4):
            for xx in range(4):
                part = total[zz * 256 + xx * 64 : zz * 256 + xx * 64 + 64]
                for buf, place, low, value in (
                    (b0, (yy, zz, xx), 0, part[:, 0:128]),
                    (b0, (yy, zz, xx), 64, part[0:24, 128:256]),
                    (b1, (zz, xx, yy), 0, part[24:64, 128:256]),
                    (b1, (zz, xx, yy), 40, part[0:48, 256:384]),
                    (b2, (xx, yy, zz), 0, part[48:64, 256:384]),
                    (b2, (xx, yy, zz), 16, part[:, 384:512]),
                ):
                    at = place + (slice(low, low + value.shape[0]),)
                    buf[at] = buf[at] + value if more else value

    loads[0].wait()
    own_part(0)
    own_part(1)
    pl.semaphore_wait(barrier, 22)

    def remote(src, dst, send, recv, device):
        return pltpu.make_async_remote_copy(
            src_ref=src,
            dst_ref=dst,
            send_sem=send,
            recv_sem=recv,
            device_id=device,
            device_id_type=MESH,
        )

    for s in range(1, 16):
        other = (fs + s) % 16
        remote(
            packed.at[:, other], middle.at[:, fs], deal_send, deal_recv, (cut, other)
        ).start()
        remote(
            second_out.at[fs], second_out.at[fs], extra_send, extra_recv, (cut, other)
        ).start()
    dealt = remote(
        packed.at[:, pl.ds(0, 15)], middle.at[:, pl.ds(0, 15)], deal_send, deal_recv, partner
    )
    seconds = remote(
        second_out.at[pl.ds(0, 15)], second_out.at[pl.ds(0, 15)], extra_send, extra_recv, partner
    )

    pairs = [remote(cotangent, c_pair, pair_send.at[4], pair_recv.at[4], partner)]
    pairs[0].start()
    for i, yy in enumerate(order):
        cols = pl.multiple_of(yy * 2048 + (1 - core) * 1024, 1024)
        copy = remote(
            hidden.at[:, pl.ds(cols, 1024)],
            h_pair.at[i],
            pair_send.at[i],
            pair_recv.at[i],
            partner,
        )
        copy.start()
        pairs.append(copy)

    bufs, fars, nears = (b0, b1, b2), (f0, f1, f2), (n0, n1, n2)

    class Stage:
        def __init__(self, colour, phase):
            self.axis = ORDER[colour][phase]
            self.mine = here[self.axis]
            index = tuple(here[a] for a in ORDER[colour][:phase])
            self.buf = bufs[colour].at[index] if phase else bufs[colour]
            self.phase = phase
            rows = ROWS[colour]
            if phase == 0:
                self.halves = ((pl.ds(0, 2),), (pl.ds(2, 2),))
            elif phase == 1:
                self.halves = ((pl.ds(0, 2),), (pl.ds(2, 2),))
            else:
                cut_at = SPLIT[colour]
                self.halves = ((pl.ds(0, cut_at),), (pl.ds(cut_at, rows - cut_at),))
            self.far = [fars[colour][phase].at[d] for d in range(2)]
            if phase == 2:
                self.far = [fars[colour][phase].at[d, h[0]] for d, h in enumerate(self.halves)]
            self.near = [nears[colour][phase].at[d] for d in range(2)]
            base = (colour * 3 + phase) * 6
            self.copies = []
            for d, step in enumerate((1, -1)):
                to = neighbour(self.axis, step)
                far = self.buf.at[((self.mine + 2) % 4,) + self.halves[d]]
                close = (self.mine + step) % 4
                own = self.buf.at[(close,) + self.halves[1 - d]]
                acc = self.buf.at[(close,) + self.halves[d]]
                self.copies.append(
                    (
                        remote(far, self.far[d], ring_send.at[base + d], ring_recv.at[base + d], to),
                        remote(
                            own,
                            self.near[d].at[self.halves[1 - d]],
                            ring_send.at[base + 2 + d],
                            ring_recv.at[base + 2 + d],
                            to,
                        ),
                        remote(
                            acc,
                            self.near[d].at[self.halves[d]],
                            ring_send.at[base + 4 + d],
                            ring_recv.at[base + 4 + d],
                            to,
                        ),
                        acc,
                    )
                )

            self.split = []
            if phase == 0 and colour:
                for i, yy in enumerate(order):
                    if colour == 1:
                        for d, step in enumerate((1, -1)):
                            k = i * 2 + d
                            self.split.append(
                                remote(
                                    self.buf.at[((self.mine + 2) % 4,) + self.halves[d] + (yy,)],
                                    self.far[d].at[pl.ds(0, 2), yy],
                                    far_send.at[k],
                                    far_recv.at[k],
                                    neighbour(self.axis, step),
                                )
                            )
                    else:
                        k = 8 + i
                        d = yy // 2
                        self.split.append(
                            remote(
                                self.buf.at[(self.mine + 2) % 4, yy],
                                fars[colour][0].at[d, yy % 2],
                                far_send.at[k],
                                far_recv.at[k],
                                neighbour(self.axis, 1 - 2 * d),
                            )
                        )

        def add(self, target, parts):
            if self.phase == 0:
                add_into(target, parts)
            elif self.phase == 1:
                for i in range(target.shape[0]):
                    total = target[i]
                    for part in parts:
                        total = total + part[i]
                    target[i] = total
            else:
                total = target[...]
                for part in parts:
                    total = total + part[...]
                target[...] = total

        def far_out(self):
            for d in range(2):
                self.copies[d][0].start()

        def far_part(self, i):
            n = len(self.split) // 4
            for c in self.split[i * n : i * n + n]:
                c.start()

        def own_out(self):
            for d in range(2):
                self.copies[d][1].start()

        def middle(self):
            for c in self.split:
                c.wait_recv()
            for d in range(2):
                far, _, onward, acc = self.copies[d]
                if not self.split:
                    far.wait_recv()
                self.add(acc, [self.far[d]])
                onward.start()

        def finish(self):
            for d in range(2):
                self.copies[d][1].wait_recv()
                self.copies[d][2].wait_recv()
            self.add(self.buf.at[self.mine], self.near)

        def drain(self):
            for c in self.split:
                c.wait_send()
            for d in range(2):
                for c in range(1 if self.split else 0, 3):
                    self.copies[d][c].wait_send()

    class Turn:
        def __init__(self, colour, phase):
            self.colour, self.phase = colour, phase
            self.axis = ORDER[colour][phase]
            self.mine = here[self.axis]
            pieces = range(4) if phase == 2 else (None,)
            base = (0, 12, 24)[phase] + colour * (12 if phase == 2 else 4)
            self.begun, self.onward = ([], []), ([], [])
            for d, step in enumerate((1, -1)):
                to = neighbour(self.axis, step)
                for piece in pieces if d == 0 or phase < 2 else (2, 3, 0, 1):
                    own = self.region(self.mine, piece=piece)
                    self.begun[d].append(
                        remote(own, own, turn_send.at[base], turn_recv.at[base], to)
                    )
                    base += 1
                for piece in ((0, 1), (2, 3))[d] if phase == 2 else (None,):
                    other = self.region((self.mine - step) % 4, d if phase < 2 else None, piece)
                    self.onward[d].append(
                        remote(other, other, turn_send.at[base], turn_recv.at[base], to)
                    )
                    base += 1

        def region(self, index, half=None, piece=None):
            place = list(here)
            for a in ORDER[self.colour][: self.phase]:
                place[a] = pl.ds(0, 4)
            place[self.axis] = index
            cols = pl.ds(0, 512)
            if half is not None and self.phase == 0:
                cols = pl.ds(half * 256, 256)
            elif half is not None:
                place[ORDER[self.colour][0]] = pl.ds(half * 2, 2)
            if piece is not None:
                place[ORDER[self.colour][0]] = piece
            rows = pl.ds(W_FIRST[self.colour], W_ROWS[self.colour])
            return whole.at[place[0], core, place[1], place[2], rows, cols]

        def begin(self, n=0):
            for d in range(2):
                self.begun[d][n].start()

        def middle(self, n=0):
            for d in range(2):
                self.begun[d][n].wait_recv()
                self.onward[d][n].start()

        def arrive(self, n):
            for d in range(2):
                self.begun[d][n].wait_recv()

        def finish(self, n=0):
            for d in range(2):
                self.onward[d][n].wait_recv()

        def drain(self):
            for d in range(2):
                for c in self.begun[d] + self.onward[d]:
                    c.wait_send()

    def hand(turn, index, n):
        slab = turn.region(index)
        k = turn.colour * 4 + n
        return remote(slab, slab, pass_send.at[k], pass_recv.at[k], partner)

    stages = [[Stage(colour, phase) for colour in range(3)] for phase in range(3)]
    turns = [[Turn(colour, phase) for colour in range(3)] for phase in range(3)]

    def each(things, step, *given):
        for thing in things:
            getattr(thing, step)(*given)

    def unpack():
        lined.wait_recv()
        seconds_lined.wait_recv()
        table[...] = arrived[...].reshape(1024, 128).astype(f32)
        side = table[pl.ds(6, 128, stride=8), :]
        mark = jnp.sum(jnp.where(row == col, side[:, 6:7], 0.0), axis=0, keepdims=True)
        counted = jnp.sum(jnp.where(row == col, side[:, 7:8], 0.0), axis=0, keepdims=True)
        before = jnp.sum(jnp.where(row < col, side[:, 7:8], 0.0), axis=0, keepdims=True)
        after = jnp.sum(jnp.where(counted > 1.5, before + 1.0, 0.0), axis=1, keepdims=True)
        tile = second_last[0].astype(f32)
        for n in range(1, 8):
            tile = tile + second_last[n].astype(f32)
        blocks = jnp.concatenate(
            [table[pl.ds(q, 128, stride=8), :].astype(b16) for q in range(7)], axis=1
        )
        new_row = row[0:64].astype(f32)
        for h in range(2):
            choose = (before == 2.0 * new_row + h) & (mark > 0.5)
            got = jnp.dot(
                jnp.where(choose, 1.0, 0.0).astype(b16), blocks, preferred_element_type=f32
            )
            here_too = 2.0 * new_row + h == after
            for q in range(7):
                cols = slice(q * 128, q * 128 + 128)
                owned[h, :, cols] = got[:, cols] + jnp.where(here_too, tile[q : q + 1, :], 0.0)
            whole[y, core, z, x, :, h * 256 : h * 256 + 256] = owned[h, :, 0:256].astype(b16)

    own_part(2)
    own_part(3)
    dealt.wait_recv()
    seconds.wait_recv()
    arrived[cut] = middle[cut]
    held = [second_out[n].astype(f32) for n in range(16)]
    for c in range(8):
        wanted = (fs + c * 16).astype(f32)
        tile = jnp.zeros((8, 128), f32)
        for n in range(16):
            tile = tile + jnp.where(held[n][6:7, 7:8] == wanted, held[n], 0.0)
        second_mid[c] = tile.astype(b16)
    second_last[cut] = second_mid[cut]
    for s in range(1, 8):
        other = (cut + s) % 8
        remote(middle.at[other], arrived.at[cut], line_send, line_recv, (other, fs)).start()
        remote(
            second_mid.at[other], second_last.at[cut], extra_line_send, extra_line_recv, (other, fs)
        ).start()
    lined = remote(
        middle.at[pl.ds(0, 7)], arrived.at[pl.ds(0, 7)], line_send, line_recv, partner
    )
    seconds_lined = remote(
        second_mid.at[pl.ds(0, 7)],
        second_last.at[pl.ds(0, 7)],
        extra_line_send,
        extra_line_recv,
        partner,
    )
    pairs[0].wait_recv()
    pair_part(0)
    each(stages[0][:1], "far_out")
    each(stages[0][1:], "far_part", 0)
    pair_part(1)
    each(stages[0][1:], "far_part", 1)
    pair_part(2)
    each(stages[0][1:], "far_part", 2)
    each(stages[0][:1], "own_out")
    pair_part(3)
    each(stages[0][1:], "far_part", 3)
    each(stages[0][1:], "own_out")
    unpack()
    each(turns[0], "begin")
    each(stages[0], "middle")
    each(turns[0], "middle")
    each(turns[0], "finish")
    each(turns[1], "begin")
    each(stages[0], "finish")
    each(stages[1], "far_out")
    each(stages[1], "own_out")
    each(turns[1], "middle")
    each(stages[1], "middle")
    each(turns[1], "finish")
    each(turns[2], "begin", 0)
    passes = [hand(t, t.mine, 0) for t in turns[2]]
    for p in passes:
        p.start()
    each(stages[1], "finish")
    each(stages[2], "far_out")
    each(stages[2], "own_out")
    each(turns[2], "begin", 1)
    each(turns[2], "middle", 0)
    each(stages[2], "middle")
    each(turns[2], "begin", 2)
    each(stages[2], "finish")

    for colour in range(3):
        index = tuple(here[a] for a in ORDER[colour])
        grad[FIRST[colour] : FIRST[colour] + ROWS[colour], :] = bufs[colour][index] * (1.0 / 65536)

    g = grad[...]
    squares = jnp.sum((g * g).reshape(32, 8, 128), axis=0)

    def tell(board, mine, count, base, target):
        copies = [
            remote(
                board.at[mine], board.at[mine], sum_send.at[base + s], sum_recv.at[base + s], target(s)
            )
            for s in range(1, count)
        ]
        for c in copies:
            c.start()
        return copies

    def hear(board, count, copies):
        for c in copies:
            c.wait()
        total = board[0]
        for s in range(1, count):
            total = total + board[s]
        return total

    plane[fs] = squares
    told = tell(plane, fs, 16, 0, lambda s: (cut, (fs + s) % 16))
    each(turns[2], "begin", 3)
    each(turns[2], "middle", 1)
    for t in turns[2]:
        t.arrive(2)
        t.arrive(3)
        for n, step in ((1, -1), (2, 1)):
            p = hand(t, (t.mine + step) % 4, n)
            p.start()
            passes.append(p)
    squares = hear(plane, 16, told)
    line[cut] = squares
    told = tell(line, cut, 8, 16, lambda s: ((cut + s) % 8, fs))
    for t in turns[2]:
        t.finish(0)
        t.finish(1)
        p = hand(t, (t.mine + 2) % 4, 3)
        p.start()
        passes.append(p)
    squares = hear(line, 8, told)
    norm = jnp.sqrt(jnp.sum(squares, keepdims=True))
    factor = jnp.minimum(1.0, clip_norm / (norm + 1e-06))

    eye = lax.broadcasted_iota(jnp.int32, (64, 64), 0) == lax.broadcasted_iota(
        jnp.int32, (64, 64), 1
    )
    for h in range(2):
        m_new, v_new = [], []
        m_by = owned[h, :, 768:769] + owned[h, :, 769:770] + owned[h, :, 770:771]
        v_by = owned[h, :, 771:772] + owned[h, :, 772:773] + owned[h, :, 773:774]
        for n in range(2):
            j = 2 * h + n
            cols = slice(j * 128, j * 128 + 128)
            clipped = grad[j * 64 : j * 64 + 64, :] * factor
            m_old = owned[h, :, 256 + n * 128 : 384 + n * 128] * m_by
            v_old = owned[h, :, 512 + n * 128 : 640 + n * 128] * v_by
            m = beta_first * m_old + (1.0 - beta_first) * clipped
            v = beta_second * v_old + (1.0 - beta_second) * clipped * clipped
            m_hat = m / (1.0 - beta_first**STEP)
            v_hat = v / (1.0 - beta_second**STEP)
            w_old = owned[h, :, n * 128 : n * 128 + 128]
            w_out[:, cols] = (
                w_old
                - learn_rate * (m_hat / (jnp.sqrt(v_hat) + adam_epsilon) + weight_decay * w_old)
            ).astype(b16)
            m_new.append(m)
            v_new.append(v)
        m_scale = (
            jnp.max(jnp.maximum(jnp.abs(m_new[0]), jnp.abs(m_new[1])), axis=1, keepdims=True)
            + tiny_scale
        )
        v_scale = jnp.max(jnp.maximum(v_new[0], v_new[1]), axis=1, keepdims=True) + tiny_scale
        ms_out[h : h + 1, :] = jnp.sum(jnp.where(eye, m_scale, 0.0), axis=0, keepdims=True)
        vs_out[h : h + 1, :] = jnp.sum(jnp.where(eye, v_scale, 0.0), axis=0, keepdims=True)
        for n in range(2):
            cols = slice((2 * h + n) * 128, (2 * h + n) * 128 + 128)
            m_out[:, cols] = (m_new[n] / m_scale).astype(b16)
            v_out[:, cols] = (v_new[n] / v_scale).astype(b16)

    for p in passes:
        p.wait()
    for c in pairs:
        c.wait_send()
    lined.wait_send()
    seconds.wait_send()
    seconds_lined.wait_send()
    dealt.wait_send()
    for group in stages + turns:
        each(group, "drain")


def main_call(*given):
    vmem = pl.BlockSpec(memory_space=pltpu.VMEM)
    hbm = pl.BlockSpec(memory_space=pltpu.HBM)
    f32, b16 = jnp.float32, jnp.bfloat16
    scratch = [
        pltpu.VMEM((4, 512, 1024), b16),
        pltpu.VMEM((4, 512, 1024), b16),
        pltpu.VMEM((512, 512), b16),
    ]
    scratch += [pltpu.VMEM((4, 4, 4, r, 128), f32) for r in ROWS]
    scratch += [
        [
            pltpu.VMEM((2, 2, 4, r, 128), f32),
            pltpu.VMEM((2, 2, r, 128), f32),
            pltpu.VMEM((2, r, 128), f32),
        ]
        for r in ROWS
    ]
    scratch += [
        [
            pltpu.VMEM((2, 4, 4, r, 128), f32),
            pltpu.VMEM((2, 4, r, 128), f32),
            pltpu.VMEM((2, r, 128), f32),
        ]
        for r in ROWS
    ]
    scratch += [
        pltpu.VMEM((256, 128), f32),
        pltpu.VMEM((16, 8, 128), f32),
        pltpu.VMEM((8, 8, 128), f32),
        pltpu.VMEM((1024, 128), f32),
        pltpu.VMEM((8, 16, 8, 128), b16),
        pltpu.VMEM((8, 16, 8, 128), b16),
        pltpu.VMEM((8, 16, 8, 128), b16),
        pltpu.VMEM((16, 8, 128), b16),
        pltpu.VMEM((8, 8, 128), b16),
        pltpu.VMEM((8, 8, 128), b16),
        pltpu.VMEM((2, 64, 896), f32),
        pltpu.VMEM((128, 256), b16),
        pltpu.VMEM((128, 256), b16),
        pltpu.VMEM((128, 256), b16),
        pltpu.VMEM((1, 128), f32),
        pltpu.VMEM((1, 128), f32),
        pltpu.VMEM((1, 128), jnp.int32),
        pltpu.SemaphoreType.DMA((11,)),
        pltpu.SemaphoreType.DMA((5,)),
        pltpu.SemaphoreType.DMA((5,)),
        pltpu.SemaphoreType.DMA((54,)),
        pltpu.SemaphoreType.DMA((54,)),
        pltpu.SemaphoreType.DMA((12,)),
        pltpu.SemaphoreType.DMA((12,)),
        pltpu.SemaphoreType.DMA((24,)),
        pltpu.SemaphoreType.DMA((24,)),
        pltpu.SemaphoreType.DMA,
        pltpu.SemaphoreType.DMA,
        pltpu.SemaphoreType.DMA,
        pltpu.SemaphoreType.DMA,
        pltpu.SemaphoreType.DMA,
        pltpu.SemaphoreType.DMA,
        pltpu.SemaphoreType.DMA,
        pltpu.SemaphoreType.DMA,
        pltpu.SemaphoreType.DMA((60,)),
        pltpu.SemaphoreType.DMA((60,)),
        pltpu.SemaphoreType.DMA((12,)),
        pltpu.SemaphoreType.DMA((12,)),
    ]
    return pl.pallas_call(
        main_kernel,
        out_shape=(
            pltpu.VMEM((4, 2, 4, 4, 64, 512), b16),
            pltpu.VMEM((512, 512), b16),
            pltpu.VMEM((64, 512), b16),
            pltpu.VMEM((64, 512), b16),
            pltpu.VMEM((2, 64), f32),
            pltpu.VMEM((64, 512), b16),
            pltpu.VMEM((2, 64), f32),
        ),
        in_specs=[hbm] * 8,
        out_specs=(vmem,) * 7,
        scratch_shapes=scratch,
        compiler_params=pltpu.CompilerParams(
            collective_id=0, has_side_effects=True, vmem_limit_bytes=57_400_000
        ),
        name="exchange_adam",
    )(*given)


def last_kernel(cotangent, weight, *refs):
    given, (out, *kept), (slab, sems) = refs[:5], refs[5:11], refs[11:]
    copies = []
    for y in range(4):
        for core in range(2):
            i = y * 2 + core
            slab[i] = lax.dot_general(
                cotangent[...],
                weight[y, core].reshape(1024, 512),
                (((1,), (1,)), ((), ())),
                preferred_element_type=jnp.float32,
            ).astype(jnp.bfloat16)
            copies.append(
                pltpu.make_async_copy(
                    slab.at[i], out.at[:, pl.ds(i * 1024, 1024)], sems.at[i]
                )
            )
            copies[-1].start()
    for a, b in zip(given, kept):
        b[...] = a[...]
    for c in copies:
        c.wait()


def last_call(cotangent, weight, small):
    vmem = pl.BlockSpec(memory_space=pltpu.VMEM)
    held = [pltpu.with_memory_space_constraint(a, pltpu.VMEM) for a in (cotangent, weight, *small)]
    return pl.pallas_call(
        last_kernel,
        out_shape=[jax.ShapeDtypeStruct((512, 8192), jnp.bfloat16)]
        + [jax.ShapeDtypeStruct(a.shape, a.dtype) for a in small],
        in_specs=[vmem] * 7,
        out_specs=[pl.BlockSpec(memory_space=pl.ANY)] + [vmem] * 5,
        scratch_shapes=[pltpu.VMEM((8, 512, 1024), jnp.bfloat16), pltpu.SemaphoreType.DMA((8,))],
        compiler_params=pltpu.CompilerParams(vmem_limit_bytes=24_000_000),
        name="input_grad",
    )(*held)


def shards(
    hidden_states,
    key_cotangent,
    old_weight,
    old_first,
    old_first_scale,
    old_second,
    old_second_scale,
    send_counts,
):
    gathered, cotangent, *small = main_call(
        hidden_states, key_cotangent, old_weight, old_first, old_second,
        old_first_scale[None], old_second_scale[None], send_counts,
    )
    input_grad, w_new, m_code, m_scale, v_code, v_scale = last_call(
        cotangent, gathered, small
    )
    return (input_grad, w_new, m_code, m_scale.T, v_code, v_scale.T)


def solution(mesh):
    rows = P(AXES, None)
    placed = (rows, rows, rows, rows, P(AXES), rows, P(AXES), rows)
    return jax.shard_map(
        shards, mesh=mesh, in_specs=placed, out_specs=(rows,) * 6, check_vma=False
    )
```

```python
import jax
import jax.numpy as jnp
from jax import lax
from jax.experimental import pallas as pl
from jax.experimental.pallas import tpu as pltpu
from jax.sharding import PartitionSpec as P

STEP = 2000

beta_first = 0.9
beta_second = 0.95
adam_epsilon = 1e-05
learn_rate = 0.001
weight_decay = 0.1
clip_norm = 1.0
tiny_scale = 1e-30

ROWS_OUT = (((0,), (0,)), ((), ()))
AXES = ("cuts", "fsdp")
MESH = pl.DeviceIdType.MESH
ROWS = (88, 88, 80)
FIRST = (0, 88, 176)
ORDER = ((0, 1, 2), (1, 2, 0), (2, 0, 1))
SPLIT = (48, 48, 40)
W_ROWS = (24, 24, 16)
W_FIRST = (0, 24, 48)


def add_into(target, parts):
    outer, inner = target.shape[:2]

    def body(i, carry):
        a, b = i // inner, i % inner
        total = target[a, b]
        for part in parts:
            total = total + part[a, b]
        target[a, b] = total
        return carry

    lax.fori_loop(0, outer * inner, body, 0)


def main_kernel(
    hidden,
    cotangent,
    weight_in,
    first_in,
    second_in,
    first_by_in,
    second_by_in,
    counts_in,
    whole,
    c_own,
    w_out,
    m_out,
    ms_out,
    v_out,
    vs_out,
    h_own,
    h_pair,
    c_pair,
    b0,
    b1,
    b2,
    f0,
    f1,
    f2,
    n0,
    n1,
    n2,
    grad,
    plane,
    line,
    table,
    packed,
    middle,
    arrived,
    second_out,
    second_mid,
    second_last,
    owned,
    weight,
    first,
    second,
    first_by,
    second_by,
    counts,
    load_sem,
    pair_send,
    pair_recv,
    ring_send,
    ring_recv,
    far_send,
    far_recv,
    sum_send,
    sum_recv,
    deal_send,
    deal_recv,
    line_send,
    line_recv,
    extra_send,
    extra_recv,
    extra_line_send,
    extra_line_recv,
    turn_send,
    turn_recv,
    pass_send,
    pass_recv,
):
    cut = lax.axis_index("cuts")
    fs = lax.axis_index("fsdp")
    y, core = cut // 2, cut % 2
    z, x = fs // 4, fs % 4
    here = (y, z, x)

    def at(y, z, x, core):
        return (y * 2 + core, z * 4 + x)

    def neighbour(axis, step):
        place = list(here)
        place[axis] = (place[axis] + step) % 4
        return at(*place, core)

    partner = at(y, z, x, 1 - core)

    order = [(y + s) % 4 for s in (2, 1, 3, 0)]
    state = [
        pltpu.make_async_copy(a, b, load_sem.at[5 + n])
        for n, (a, b) in enumerate(
            (
                (weight_in, weight),
                (first_in, first),
                (second_in, second),
                (first_by_in, first_by),
                (second_by_in, second_by),
                (counts_in, counts),
            )
        )
    ]
    for copy in state:
        copy.start()
    loads = [pltpu.make_async_copy(cotangent, c_own, load_sem.at[4])]
    loads[0].start()
    for i, yy in enumerate(order):
        cols = pl.multiple_of(yy * 2048 + core * 1024, 1024)
        copy = pltpu.make_async_copy(hidden.at[:, pl.ds(cols, 1024)], h_own.at[i], load_sem.at[i])
        copy.start()
        loads.append(copy)

    f32, b16 = jnp.float32, jnp.bfloat16
    barrier = pltpu.get_barrier_semaphore()

    for s in range(1, 16):
        pl.semaphore_signal(barrier, inc=1, device_id=(cut, (fs + s) % 16), device_id_type=MESH)
    for s in range(1, 8):
        pl.semaphore_signal(barrier, inc=1, device_id=((cut + s) % 8, fs), device_id_type=MESH)

    row = lax.broadcasted_iota(jnp.int32, (128, 128), 0)
    col = lax.broadcasted_iota(jnp.int32, (128, 128), 1)
    for copy in state:
        copy.wait()
    mine = counts[...]
    starts = jnp.sum(jnp.where(col < row, mine, 0).astype(f32), axis=1, keepdims=True)
    amount = jnp.sum(jnp.where(col == row, mine, 0).astype(f32), axis=1, keepdims=True)
    slot = col.astype(f32)
    values = jnp.concatenate([weight[...], first[...], second[...]], axis=1)
    table[...] = jnp.zeros_like(table)

    def sided(pick, rows, seven):
        side = jnp.where(rows == 6, 1.0, 0.0) * jnp.sum(pick, axis=1, keepdims=True)
        side = side + jnp.where(rows == 7, seven, 0.0)
        for n, by in enumerate((first_by, second_by)):
            rest = jnp.sum(pick * by[...], axis=1, keepdims=True)
            for part in range(3):
                high = rest.astype(b16).astype(f32)
                side = side + jnp.where(rows == n * 3 + part, high, 0.0)
                rest = rest - high
        return side

    pick = jnp.where((slot == starts) & (amount > 0), 1.0, 0.0)
    chosen = jnp.dot(pick.astype(b16), values, preferred_element_type=f32)
    for q in range(6):
        table[pl.ds(q, 128, stride=8), :] = chosen[:, q * 128 : q * 128 + 128]
    table[pl.ds(6, 128, stride=8), :] = sided(pick, col, amount)
    packed[...] = table[...].astype(b16).reshape(8, 16, 8, 128)
    middle[:, fs] = packed[:, fs]
    twice = amount > 1
    pick = jnp.sum(jnp.where(twice & (slot == starts + 1), 1.0, 0.0), axis=0, keepdims=True)
    owner = jnp.sum(
        jnp.where(twice, row[:, 0:1].astype(f32), 0.0), axis=0, keepdims=True
    )
    pick = jnp.broadcast_to(pick, (8, 128))
    chosen = jnp.dot(pick.astype(b16), values, preferred_element_type=f32)
    eight = row[0:8]
    extra = jnp.where(eight == 6, sided(pick, col[0:8], owner), 0.0)
    for q in range(6):
        extra = extra + jnp.where(eight == q, chosen[:, q * 128 : q * 128 + 128], 0.0)
    second_out[fs] = extra.astype(b16)

    def own_part(i):
        loads[1 + i].wait()
        spread(i, lax.dot_general(h_own[i], c_own[...], ROWS_OUT, preferred_element_type=f32), False)

    def pair_part(i):
        pairs[1 + i].wait_recv()
        spread(i, lax.dot_general(h_pair[i], c_pair[...], ROWS_OUT, preferred_element_type=f32), True)

    def spread(i, total, more):
        yy = order[i]
        for zz in range(4):
            for xx in range(4):
                part = total[zz * 256 + xx * 64 : zz * 256 + xx * 64 + 64]
                for buf, place, low, value in (
                    (b0, (yy, zz, xx), 0, part[:, 0:128]),
                    (b0, (yy, zz, xx), 64, part[0:24, 128:256]),
                    (b1, (zz, xx, yy), 0, part[24:64, 128:256]),
                    (b1, (zz, xx, yy), 40, part[0:48, 256:384]),
                    (b2, (xx, yy, zz), 0, part[48:64, 256:384]),
                    (b2, (xx, yy, zz), 16, part[:, 384:512]),
                ):
                    at = place + (slice(low, low + value.shape[0]),)
                    buf[at] = buf[at] + value if more else value

    loads[0].wait()
    own_part(0)
    own_part(1)
    pl.semaphore_wait(barrier, 22)

    def remote(src, dst, send, recv, device):
        return pltpu.make_async_remote_copy(
            src_ref=src,
            dst_ref=dst,
            send_sem=send,
            recv_sem=recv,
            device_id=device,
            device_id_type=MESH,
        )

    for s in range(1, 16):
        other = (fs + s) % 16
        remote(
            packed.at[:, other], middle.at[:, fs], deal_send, deal_recv, (cut, other)
        ).start()
        remote(
            second_out.at[fs], second_out.at[fs], extra_send, extra_recv, (cut, other)
        ).start()
    dealt = remote(
        packed.at[:, pl.ds(0, 15)], middle.at[:, pl.ds(0, 15)], deal_send, deal_recv, partner
    )
    seconds = remote(
        second_out.at[pl.ds(0, 15)], second_out.at[pl.ds(0, 15)], extra_send, extra_recv, partner
    )

    pairs = [remote(cotangent, c_pair, pair_send.at[4], pair_recv.at[4], partner)]
    pairs[0].start()
    for i, yy in enumerate(order):
        cols = pl.multiple_of(yy * 2048 + (1 - core) * 1024, 1024)
        copy = remote(
            hidden.at[:, pl.ds(cols, 1024)],
            h_pair.at[i],
            pair_send.at[i],
            pair_recv.at[i],
            partner,
        )
        copy.start()
        pairs.append(copy)

    bufs, fars, nears = (b0, b1, b2), (f0, f1, f2), (n0, n1, n2)

    class Stage:
        def __init__(self, colour, phase):
            self.axis = ORDER[colour][phase]
            self.mine = here[self.axis]
            index = tuple(here[a] for a in ORDER[colour][:phase])
            self.buf = bufs[colour].at[index] if phase else bufs[colour]
            self.phase = phase
            rows = ROWS[colour]
            if phase == 0:
                self.halves = ((pl.ds(0, 2),), (pl.ds(2, 2),))
            elif phase == 1:
                self.halves = ((pl.ds(0, 2),), (pl.ds(2, 2),))
            else:
                cut_at = SPLIT[colour]
                self.halves = ((pl.ds(0, cut_at),), (pl.ds(cut_at, rows - cut_at),))
            self.far = [fars[colour][phase].at[d] for d in range(2)]
            if phase == 2:
                self.far = [fars[colour][phase].at[d, h[0]] for d, h in enumerate(self.halves)]
            self.near = [nears[colour][phase].at[d] for d in range(2)]
            base = (colour * 3 + phase) * 6
            self.copies = []
            for d, step in enumerate((1, -1)):
                to = neighbour(self.axis, step)
                far = self.buf.at[((self.mine + 2) % 4,) + self.halves[d]]
                close = (self.mine + step) % 4
                own = self.buf.at[(close,) + self.halves[1 - d]]
                acc = self.buf.at[(close,) + self.halves[d]]
                self.copies.append(
                    (
                        remote(far, self.far[d], ring_send.at[base + d], ring_recv.at[base + d], to),
                        remote(
                            own,
                            self.near[d].at[self.halves[1 - d]],
                            ring_send.at[base + 2 + d],
                            ring_recv.at[base + 2 + d],
                            to,
                        ),
                        remote(
                            acc,
                            self.near[d].at[self.halves[d]],
                            ring_send.at[base + 4 + d],
                            ring_recv.at[base + 4 + d],
                            to,
                        ),
                        acc,
                    )
                )

            self.split = []
            if phase == 0 and colour:
                for i, yy in enumerate(order):
                    if colour == 1:
                        for d, step in enumerate((1, -1)):
                            k = i * 2 + d
                            self.split.append(
                                remote(
                                    self.buf.at[((self.mine + 2) % 4,) + self.halves[d] + (yy,)],
                                    self.far[d].at[pl.ds(0, 2), yy],
                                    far_send.at[k],
                                    far_recv.at[k],
                                    neighbour(self.axis, step),
                                )
                            )
                    else:
                        k = 8 + i
                        d = yy // 2
                        self.split.append(
                            remote(
                                self.buf.at[(self.mine + 2) % 4, yy],
                                fars[colour][0].at[d, yy % 2],
                                far_send.at[k],
                                far_recv.at[k],
                                neighbour(self.axis, 1 - 2 * d),
                            )
                        )

        def add(self, target, parts):
            if self.phase == 0:
                add_into(target, parts)
            elif self.phase == 1:
                for i in range(target.shape[0]):
                    total = target[i]
                    for part in parts:
                        total = total + part[i]
                    target[i] = total
            else:
                total = target[...]
                for part in parts:
                    total = total + part[...]
                target[...] = total

        def far_out(self):
            for d in range(2):
                self.copies[d][0].start()

        def far_part(self, i):
            n = len(self.split) // 4
            for c in self.split[i * n : i * n + n]:
                c.start()

        def own_out(self):
            for d in range(2):
                self.copies[d][1].start()

        def middle(self):
            for c in self.split:
                c.wait_recv()
            for d in range(2):
                far, _, onward, acc = self.copies[d]
                if not self.split:
                    far.wait_recv()
                self.add(acc, [self.far[d]])
                onward.start()

        def finish(self):
            for d in range(2):
                self.copies[d][1].wait_recv()
                self.copies[d][2].wait_recv()
            self.add(self.buf.at[self.mine], self.near)

        def drain(self):
            for c in self.split:
                c.wait_send()
            for d in range(2):
                for c in range(1 if self.split else 0, 3):
                    self.copies[d][c].wait_send()

    class Turn:
        def __init__(self, colour, phase):
            self.colour, self.phase = colour, phase
            self.axis = ORDER[colour][phase]
            self.mine = here[self.axis]
            pieces = range(4) if phase == 2 else (None,)
            base = (0, 12, 24)[phase] + colour * (12 if phase == 2 else 4)
            self.begun, self.onward = ([], []), ([], [])
            for d, step in enumerate((1, -1)):
                to = neighbour(self.axis, step)
                for piece in pieces if d == 0 or phase < 2 else (2, 3, 0, 1):
                    own = self.region(self.mine, piece=piece)
                    self.begun[d].append(
                        remote(own, own, turn_send.at[base], turn_recv.at[base], to)
                    )
                    base += 1
                for piece in ((0, 1), (2, 3))[d] if phase == 2 else (None,):
                    other = self.region((self.mine - step) % 4, d if phase < 2 else None, piece)
                    self.onward[d].append(
                        remote(other, other, turn_send.at[base], turn_recv.at[base], to)
                    )
                    base += 1

        def region(self, index, half=None, piece=None):
            place = list(here)
            for a in ORDER[self.colour][: self.phase]:
                place[a] = pl.ds(0, 4)
            place[self.axis] = index
            cols = pl.ds(0, 512)
            if half is not None and self.phase == 0:
                cols = pl.ds(half * 256, 256)
            elif half is not None:
                place[ORDER[self.colour][0]] = pl.ds(half * 2, 2)
            if piece is not None:
                place[ORDER[self.colour][0]] = piece
            rows = pl.ds(W_FIRST[self.colour], W_ROWS[self.colour])
            return whole.at[place[0], core, place[1], place[2], rows, cols]

        def begin(self, n=0):
            for d in range(2):
                self.begun[d][n].start()

        def middle(self, n=0):
            for d in range(2):
                self.begun[d][n].wait_recv()
                self.onward[d][n].start()

        def arrive(self, n):
            for d in range(2):
                self.begun[d][n].wait_recv()

        def finish(self, n=0):
            for d in range(2):
                self.onward[d][n].wait_recv()

        def drain(self):
            for d in range(2):
                for c in self.begun[d] + self.onward[d]:
                    c.wait_send()

    def hand(turn, index, n):
        slab = turn.region(index)
        k = turn.colour * 4 + n
        return remote(slab, slab, pass_send.at[k], pass_recv.at[k], partner)

    stages = [[Stage(colour, phase) for colour in range(3)] for phase in range(3)]
    turns = [[Turn(colour, phase) for colour in range(3)] for phase in range(3)]

    def each(things, step, *given):
        for thing in things:
            getattr(thing, step)(*given)

    def unpack():
        lined.wait_recv()
        seconds_lined.wait_recv()
        table[...] = arrived[...].reshape(1024, 128).astype(f32)
        side = table[pl.ds(6, 128, stride=8), :]
        mark = jnp.sum(jnp.where(row == col, side[:, 6:7], 0.0), axis=0, keepdims=True)
        counted = jnp.sum(jnp.where(row == col, side[:, 7:8], 0.0), axis=0, keepdims=True)
        before = jnp.sum(jnp.where(row < col, side[:, 7:8], 0.0), axis=0, keepdims=True)
        after = jnp.sum(jnp.where(counted > 1.5, before + 1.0, 0.0), axis=1, keepdims=True)
        tile = second_last[0].astype(f32)
        for n in range(1, 8):
            tile = tile + second_last[n].astype(f32)
        blocks = jnp.concatenate(
            [table[pl.ds(q, 128, stride=8), :].astype(b16) for q in range(7)], axis=1
        )
        new_row = row[0:64].astype(f32)
        for h in range(2):
            choose = (before == 2.0 * new_row + h) & (mark > 0.5)
            got = jnp.dot(
                jnp.where(choose, 1.0, 0.0).astype(b16), blocks, preferred_element_type=f32
            )
            here_too = 2.0 * new_row + h == after
            for q in range(7):
                cols = slice(q * 128, q * 128 + 128)
                owned[h, :, cols] = got[:, cols] + jnp.where(here_too, tile[q : q + 1, :], 0.0)
            whole[y, core, z, x, :, h * 256 : h * 256 + 256] = owned[h, :, 0:256].astype(b16)

    own_part(2)
    own_part(3)
    dealt.wait_recv()
    seconds.wait_recv()
    arrived[cut] = middle[cut]
    held = [second_out[n].astype(f32) for n in range(16)]
    for c in range(8):
        wanted = (fs + c * 16).astype(f32)
        tile = jnp.zeros((8, 128), f32)
        for n in range(16):
            tile = tile + jnp.where(held[n][6:7, 7:8] == wanted, held[n], 0.0)
        second_mid[c] = tile.astype(b16)
    second_last[cut] = second_mid[cut]
    for s in range(1, 8):
        other = (cut + s) % 8
        remote(middle.at[other], arrived.at[cut], line_send, line_recv, (other, fs)).start()
        remote(
            second_mid.at[other], second_last.at[cut], extra_line_send, extra_line_recv, (other, fs)
        ).start()
    lined = remote(
        middle.at[pl.ds(0, 7)], arrived.at[pl.ds(0, 7)], line_send, line_recv, partner
    )
    seconds_lined = remote(
        second_mid.at[pl.ds(0, 7)],
        second_last.at[pl.ds(0, 7)],
        extra_line_send,
        extra_line_recv,
        partner,
    )
    pairs[0].wait_recv()
    pair_part(0)
    each(stages[0][:1], "far_out")
    each(stages[0][1:], "far_part", 0)
    pair_part(1)
    each(stages[0][1:], "far_part", 1)
    pair_part(2)
    each(stages[0][1:], "far_part", 2)
    each(stages[0][:1], "own_out")
    pair_part(3)
    each(stages[0][1:], "far_part", 3)
    each(stages[0][1:], "own_out")
    unpack()
    each(turns[0], "begin")
    each(stages[0], "middle")
    each(turns[0], "middle")
    each(turns[0], "finish")
    each(turns[1], "begin")
    each(stages[0], "finish")
    each(stages[1], "far_out")
    each(stages[1], "own_out")
    each(turns[1], "middle")
    each(stages[1], "middle")
    each(turns[1], "finish")
    passes = [hand(t, t.mine, 0) for t in turns[2]]
    for p in passes:
        p.start()
    each(turns[2], "begin", 0)
    each(stages[1], "finish")
    each(stages[2], "far_out")
    each(stages[2], "own_out")
    each(turns[2], "begin", 1)
    each(turns[2], "middle", 0)
    each(stages[2], "middle")
    each(turns[2], "begin", 2)
    each(turns[2], "begin", 3)
    each(stages[2], "finish")

    for colour in range(3):
        index = tuple(here[a] for a in ORDER[colour])
        grad[FIRST[colour] : FIRST[colour] + ROWS[colour], :] = bufs[colour][index] * (1.0 / 65536)

    g = grad[...]
    squares = jnp.sum((g * g).reshape(32, 8, 128), axis=0)

    def tell(board, mine, count, base, target):
        copies = [
            remote(
                board.at[mine], board.at[mine], sum_send.at[base + s], sum_recv.at[base + s], target(s)
            )
            for s in range(1, count)
        ]
        for c in copies:
            c.start()
        return copies

    def hear(board, count, copies):
        for c in copies:
            c.wait()
        total = board[0]
        for s in range(1, count):
            total = total + board[s]
        return total

    plane[fs] = squares
    told = tell(plane, fs, 16, 0, lambda s: (cut, (fs + s) % 16))
    each(turns[2], "middle", 1)
    for t in turns[2]:
        t.arrive(2)
        t.arrive(3)
        for n, step in ((1, -1), (2, 1)):
            p = hand(t, (t.mine + step) % 4, n)
            p.start()
            passes.append(p)
    squares = hear(plane, 16, told)
    line[cut] = squares
    told = tell(line, cut, 8, 16, lambda s: ((cut + s) % 8, fs))
    for t in turns[2]:
        t.finish(0)
        t.finish(1)
        p = hand(t, (t.mine + 2) % 4, 3)
        p.start()
        passes.append(p)
    squares = hear(line, 8, told)
    norm = jnp.sqrt(jnp.sum(squares, keepdims=True))
    factor = jnp.minimum(1.0, clip_norm / (norm + 1e-06))

    eye = lax.broadcasted_iota(jnp.int32, (64, 64), 0) == lax.broadcasted_iota(
        jnp.int32, (64, 64), 1
    )
    for h in range(2):
        m_new, v_new = [], []
        m_by = owned[h, :, 768:769] + owned[h, :, 769:770] + owned[h, :, 770:771]
        v_by = owned[h, :, 771:772] + owned[h, :, 772:773] + owned[h, :, 773:774]
        for n in range(2):
            j = 2 * h + n
            cols = slice(j * 128, j * 128 + 128)
            clipped = grad[j * 64 : j * 64 + 64, :] * factor
            m_old = owned[h, :, 256 + n * 128 : 384 + n * 128] * m_by
            v_old = owned[h, :, 512 + n * 128 : 640 + n * 128] * v_by
            m = beta_first * m_old + (1.0 - beta_first) * clipped
            v = beta_second * v_old + (1.0 - beta_second) * clipped * clipped
            m_hat = m / (1.0 - beta_first**STEP)
            v_hat = v / (1.0 - beta_second**STEP)
            w_old = owned[h, :, n * 128 : n * 128 + 128]
            w_out[:, cols] = (
                w_old
                - learn_rate * (m_hat / (jnp.sqrt(v_hat) + adam_epsilon) + weight_decay * w_old)
            ).astype(b16)
            m_new.append(m)
            v_new.append(v)
        m_scale = (
            jnp.max(jnp.maximum(jnp.abs(m_new[0]), jnp.abs(m_new[1])), axis=1, keepdims=True)
            + tiny_scale
        )
        v_scale = jnp.max(jnp.maximum(v_new[0], v_new[1]), axis=1, keepdims=True) + tiny_scale
        ms_out[h : h + 1, :] = jnp.sum(jnp.where(eye, m_scale, 0.0), axis=0, keepdims=True)
        vs_out[h : h + 1, :] = jnp.sum(jnp.where(eye, v_scale, 0.0), axis=0, keepdims=True)
        for n in range(2):
            cols = slice((2 * h + n) * 128, (2 * h + n) * 128 + 128)
            m_out[:, cols] = (m_new[n] / m_scale).astype(b16)
            v_out[:, cols] = (v_new[n] / v_scale).astype(b16)

    for p in passes:
        p.wait()
    for c in pairs:
        c.wait_send()
    lined.wait_send()
    seconds.wait_send()
    seconds_lined.wait_send()
    dealt.wait_send()
    for group in stages + turns:
        each(group, "drain")


def main_call(*given):
    vmem = pl.BlockSpec(memory_space=pltpu.VMEM)
    hbm = pl.BlockSpec(memory_space=pltpu.HBM)
    f32, b16 = jnp.float32, jnp.bfloat16
    scratch = [
        pltpu.VMEM((4, 512, 1024), b16),
        pltpu.VMEM((4, 512, 1024), b16),
        pltpu.VMEM((512, 512), b16),
    ]
    scratch += [pltpu.VMEM((4, 4, 4, r, 128), f32) for r in ROWS]
    scratch += [
        [
            pltpu.VMEM((2, 2, 4, r, 128), f32),
            pltpu.VMEM((2, 2, r, 128), f32),
            pltpu.VMEM((2, r, 128), f32),
        ]
        for r in ROWS
    ]
    scratch += [
        [
            pltpu.VMEM((2, 4, 4, r, 128), f32),
            pltpu.VMEM((2, 4, r, 128), f32),
            pltpu.VMEM((2, r, 128), f32),
        ]
        for r in ROWS
    ]
    scratch += [
        pltpu.VMEM((256, 128), f32),
        pltpu.VMEM((16, 8, 128), f32),
        pltpu.VMEM((8, 8, 128), f32),
        pltpu.VMEM((1024, 128), f32),
        pltpu.VMEM((8, 16, 8, 128), b16),
        pltpu.VMEM((8, 16, 8, 128), b16),
        pltpu.VMEM((8, 16, 8, 128), b16),
        pltpu.VMEM((16, 8, 128), b16),
        pltpu.VMEM((8, 8, 128), b16),
        pltpu.VMEM((8, 8, 128), b16),
        pltpu.VMEM((2, 64, 896), f32),
        pltpu.VMEM((128, 256), b16),
        pltpu.VMEM((128, 256), b16),
        pltpu.VMEM((128, 256), b16),
        pltpu.VMEM((1, 128), f32),
        pltpu.VMEM((1, 128), f32),
        pltpu.VMEM((1, 128), jnp.int32),
        pltpu.SemaphoreType.DMA((11,)),
        pltpu.SemaphoreType.DMA((5,)),
        pltpu.SemaphoreType.DMA((5,)),
        pltpu.SemaphoreType.DMA((54,)),
        pltpu.SemaphoreType.DMA((54,)),
        pltpu.SemaphoreType.DMA((12,)),
        pltpu.SemaphoreType.DMA((12,)),
        pltpu.SemaphoreType.DMA((24,)),
        pltpu.SemaphoreType.DMA((24,)),
        pltpu.SemaphoreType.DMA,
        pltpu.SemaphoreType.DMA,
        pltpu.SemaphoreType.DMA,
        pltpu.SemaphoreType.DMA,
        pltpu.SemaphoreType.DMA,
        pltpu.SemaphoreType.DMA,
        pltpu.SemaphoreType.DMA,
        pltpu.SemaphoreType.DMA,
        pltpu.SemaphoreType.DMA((60,)),
        pltpu.SemaphoreType.DMA((60,)),
        pltpu.SemaphoreType.DMA((12,)),
        pltpu.SemaphoreType.DMA((12,)),
    ]
    return pl.pallas_call(
        main_kernel,
        out_shape=(
            pltpu.VMEM((4, 2, 4, 4, 64, 512), b16),
            pltpu.VMEM((512, 512), b16),
            pltpu.VMEM((64, 512), b16),
            pltpu.VMEM((64, 512), b16),
            pltpu.VMEM((2, 64), f32),
            pltpu.VMEM((64, 512), b16),
            pltpu.VMEM((2, 64), f32),
        ),
        in_specs=[hbm] * 8,
        out_specs=(vmem,) * 7,
        scratch_shapes=scratch,
        compiler_params=pltpu.CompilerParams(
            collective_id=0, has_side_effects=True, vmem_limit_bytes=57_400_000
        ),
        name="exchange_adam",
    )(*given)


def last_kernel(cotangent, weight, *refs):
    given, (out, *kept), (slab, sems) = refs[:5], refs[5:11], refs[11:]
    copies = []
    for y in range(4):
        for core in range(2):
            i = y * 2 + core
            slab[i] = lax.dot_general(
                cotangent[...],
                weight[y, core].reshape(1024, 512),
                (((1,), (1,)), ((), ())),
                preferred_element_type=jnp.float32,
            ).astype(jnp.bfloat16)
            copies.append(
                pltpu.make_async_copy(
                    slab.at[i], out.at[:, pl.ds(i * 1024, 1024)], sems.at[i]
                )
            )
            copies[-1].start()
    for a, b in zip(given, kept):
        b[...] = a[...]
    for c in copies:
        c.wait()


def last_call(cotangent, weight, small):
    vmem = pl.BlockSpec(memory_space=pltpu.VMEM)
    held = [pltpu.with_memory_space_constraint(a, pltpu.VMEM) for a in (cotangent, weight, *small)]
    return pl.pallas_call(
        last_kernel,
        out_shape=[jax.ShapeDtypeStruct((512, 8192), jnp.bfloat16)]
        + [jax.ShapeDtypeStruct(a.shape, a.dtype) for a in small],
        in_specs=[vmem] * 7,
        out_specs=[pl.BlockSpec(memory_space=pl.ANY)] + [vmem] * 5,
        scratch_shapes=[pltpu.VMEM((8, 512, 1024), jnp.bfloat16), pltpu.SemaphoreType.DMA((8,))],
        compiler_params=pltpu.CompilerParams(vmem_limit_bytes=24_000_000),
        name="input_grad",
    )(*held)


def shards(
    hidden_states,
    key_cotangent,
    old_weight,
    old_first,
    old_first_scale,
    old_second,
    old_second_scale,
    send_counts,
):
    gathered, cotangent, *small = main_call(
        hidden_states, key_cotangent, old_weight, old_first, old_second,
        old_first_scale[None], old_second_scale[None], send_counts,
    )
    input_grad, w_new, m_code, m_scale, v_code, v_scale = last_call(
        cotangent, gathered, small
    )
    return (input_grad, w_new, m_code, m_scale.T, v_code, v_scale.T)


def solution(mesh):
    rows = P(AXES, None)
    placed = (rows, rows, rows, rows, P(AXES), rows, P(AXES), rows)
    return jax.shard_map(
        shards, mesh=mesh, in_specs=placed, out_specs=(rows,) * 6, check_vma=False
    )
```
